512 devices in a mesh: section: 16 (over y_hi, x), strip: 32 (over z, y_lo, core).
Axes of the slice: x: 4, y: 8 (y_hi: 4, y_lo: 2; y = y_hi * 2 + y_lo), z: 8, core: 2. Of those that a mesh axis runs over, the one named last changes fastest.
Arguments:
- images: bfloat16 [2, 128, 32, 256], P(None, 'strip'), may hold values from -6 to 6
- conv_first: bfloat16 [16, 9, 256, 256], P('section'), may hold values from -0.1875 to 0.1875
- conv_skip: bfloat16 [16, 9, 256, 256], P('section'), may hold values from -0.09375 to 0.09375
- conv_second: bfloat16 [16, 9, 256, 256], P('section'), may hold values from -0.1875 to 0.1875
- bias_first: float32 [16, 256], P('section'), may hold values from -0.8 to 0.8
- bias_second: float32 [16, 256], P('section'), may hold values from -0.8 to 0.8
Outputs:
- activations: bfloat16 [16, 2, 128, 32, 256], P('section', None, 'strip')
The draws below stay inside these ranges and needn't reach their ends.
All inputs are finite; a program needn't handle non-finite values.
Results may differ from the reference program's by a relative error of at most 0.02.
Values may be sent and summed in bfloat16 or wider, within the bound.
No kernel may reach another device: no remote copies, remote signals or barrier semaphores. Data moves between devices by JAX's collectives and lax.ppermute only.
A program may use at most 64 MiB of HBM per device.

```python
import jax
import jax.numpy as jnp

CHANNELS = 256
COLUMNS = 32
MICRO = 2
SECTIONS = 16
HEIGHT = 128


def level_of(rng, dims, pieces, least, largest):
    loudness, own = 1.0, jax.random.fold_in(rng, 6)
    for position, shards_of in pieces:
        steps = jnp.exp(jax.random.uniform(jax.random.fold_in(own, position), (shards_of,), jnp.float32, least / len(pieces), largest / len(pieces)))
        loudness = loudness * jnp.repeat(steps, dims[position] // shards_of).reshape([-1 if axis == position else 1 for axis in range(len(dims))])
    return loudness


def scatter_about(own_key, shape, deviation, reach, cuts=(), kind=jnp.bfloat16):
    array = deviation * jax.random.normal(own_key, shape, jnp.float32)
    if cuts:
        array = array * level_of(own_key, shape, cuts, -0.22, 0.18)
    return jnp.clip(array, -reach, reach).astype(kind)


def setup_inputs(seed: int = 0) -> dict:
    streams_of = jax.random.split(jax.random.key(seed), 7)
    images = scatter_about(streams_of[0], (MICRO, HEIGHT, COLUMNS, CHANNELS), 1.0, 6.0, ((1, 32),))
    conv_first = scatter_about(streams_of[1], (SECTIONS, 9, CHANNELS, CHANNELS), (9 * CHANNELS // 2) ** -0.5, 0.1875, ((0, 16),))
    conv_skip = scatter_about(streams_of[2], (SECTIONS, 9, CHANNELS, CHANNELS), (18 * CHANNELS) ** -0.5, 0.09375, ((0, 16),))
    conv_second = scatter_about(streams_of[3], (SECTIONS, 9, CHANNELS, CHANNELS), (9 * CHANNELS // 2) ** -0.5, 0.1875, ((0, 16),))
    bias_first = scatter_about(streams_of[4], (SECTIONS, CHANNELS), 0.2, 0.8, ((0, 16),), jnp.float32)
    bias_second = scatter_about(streams_of[5], (SECTIONS, CHANNELS), 0.2, 0.8, ((0, 16),), jnp.float32)
    return {"images": images, "conv_first": conv_first, "conv_skip": conv_skip, "conv_second": conv_second, "bias_first": bias_first, "bias_second": bias_second}


def convolve(feature, weight):
    height_rows = feature.shape[0]
    width_cols = feature.shape[1]
    channels = feature.shape[2]
    padded = jnp.pad(feature, ((1, 1), (1, 1), (0, 0)))
    summed = jnp.zeros((height_rows * width_cols, weight.shape[2]), jnp.float32)
    for tap_index in range(9):
        row_offset = tap_index // 3
        column_offset = tap_index % 3
        window_rows = padded[row_offset:row_offset + height_rows, column_offset:column_offset + width_cols]
        window_rows = window_rows.reshape(height_rows * width_cols, channels)
        summed = summed + jnp.dot(window_rows, weight[tap_index], preferred_element_type=jnp.float32)
    return summed.reshape(height_rows, width_cols, weight.shape[2])


def reference(images, conv_first, conv_skip, conv_second, bias_first, bias_second):
    per_section = [[] for section_index in range(SECTIONS)]
    for micro_index in range(MICRO):
        current = images[micro_index]
        for section_index in range(SECTIONS):
            preact = convolve(current, conv_first[section_index])
            if section_index >= SECTIONS // 2:
                preact = preact + convolve(per_section[SECTIONS - 1 - section_index][micro_index], conv_skip[section_index])
            hidden = jax.nn.relu(preact + bias_first[section_index]).astype(jnp.bfloat16)
            result = jax.nn.relu(convolve(hidden, conv_second[section_index]) + bias_second[section_index]).astype(jnp.bfloat16)
            per_section[section_index].append(result)
            current = result
    return jnp.stack([jnp.stack(section_list) for section_list in per_section])
```

```python
import jax
import jax.numpy as jnp
from jax import lax
from jax.experimental import pallas as pl
from jax.experimental.pallas import tpu as pltpu
from jax.sharding import PartitionSpec as P

BF16 = jnp.bfloat16
F32 = jnp.float32
ROWS = 4
COLS = 32
CH = 256
BLOCK = ROWS * COLS
TAPS = 9 * CH
HALF = TAPS // 2
SECTIONS = 16
STRIPS = 32
HEIGHT = ROWS * STRIPS
GROUPS = SECTIONS // 2
JOINT = ("section", "strip")


def place(group, micro):
    first = 4 * (group // 2)
    return first + (micro if group % 2 == 0 else 3 - micro)


def route(moves):
    pairs = []
    for source, target, shift in moves:
        for micro in range(2):
            for strip in range(STRIPS):
                if 0 <= strip + shift < STRIPS:
                    pairs.append(
                        (
                            place(source, micro) * STRIPS + strip,
                            place(target, micro) * STRIPS + strip + shift,
                        )
                    )
    return pairs


def send(block, moves):
    return lax.ppermute(block, JOINT, route(moves))


def phase_kernel(decoder):
    kinds = 3 if decoder else 2

    def kernel(*refs):
        refs = list(refs)
        info = refs.pop(0)
        xs = [refs.pop(0) for _ in range(3)]
        if decoder:
            skip_wide = [refs.pop(0) for _ in range(3)]
            skip_narrow = refs.pop(0)
        bias = refs.pop(0)
        own = [refs.pop(0) for _ in range(kinds)]
        fetched = [refs.pop(0) for _ in range(kinds)]
        swapped = [refs.pop(0) for _ in range(kinds)]
        prev0 = refs.pop(0)
        prev1 = refs.pop(0)
        out0 = refs.pop(0)
        out1 = refs.pop(0)
        weights = refs.pop(0)
        work = refs.pop(0)
        if decoder:
            skip_work = refs.pop(0)
        sems = refs.pop(0)

        active = info[0]
        parity = info[1]
        core = info[2]
        top = info[3]
        order = [0, 2, 1] if decoder else [0, 1]

        def half_copy(source, slot, half, sem):
            return pltpu.make_async_copy(
                source, weights.at[slot, pl.ds(half * HALF, HALF)], sems.at[slot, sem]
            )

        @pl.when(active == 0)
        def _():
            out0[...] = prev0[...]
            out1[...] = prev1[...]

        @pl.when(active != 0)
        def _():
            for section in range(2):
                for kind in order:
                    slot = section * kinds + kind

                    @pl.when(parity == section)
                    def _():
                        half_copy(own[kind].at[pl.ds(0, HALF)], slot, 0, 0).start()
                        half_copy(own[kind].at[pl.ds(HALF, HALF)], slot, 1, 1).start()

                    @pl.when(parity != section)
                    def _():
                        half_copy(fetched[kind], slot, core, 0).start()
                        half_copy(swapped[kind], slot, 1 - core, 1).start()

            def ready(slot):
                half_copy(fetched[0], slot, 0, 0).wait()
                half_copy(fetched[0], slot, 1, 1).wait()

            def spread(dest, at, value, rows):
                size = rows * COLS
                column = lax.broadcasted_iota(jnp.int32, (size, CH), 0) & (COLS - 1)
                left = jnp.where(column == 0, 0.0, pltpu.roll(value, 1, 0))
                right = jnp.where(column == COLS - 1, 0.0, pltpu.roll(value, size - 1, 0))
                dest[at : at + size, 0:CH] = left.astype(BF16)
                dest[at : at + size, CH : 2 * CH] = value.astype(BF16)
                dest[at : at + size, 2 * CH : 3 * CH] = right.astype(BF16)

            def conv(source, slot, rows):
                size = rows * COLS
                total = None
                for tap in range(3):
                    part = jnp.dot(
                        source[tap * COLS : tap * COLS + size, :],
                        weights[slot, tap * 3 * CH : (tap + 1) * 3 * CH, :],
                        preferred_element_type=F32,
                    )
                    total = part if total is None else total + part
                return total

            def finish(total, which, rows, start):
                size = rows * COLS
                value = jnp.maximum(total + bias[which : which + 1, :], 0.0)
                row = (lax.broadcasted_iota(jnp.int32, (size, CH), 0) >> 5) + (top + start)
                value = jnp.where((row >= 0) & (row < HEIGHT), value, 0.0)
                return value.astype(BF16).astype(F32)

            for index, ref in enumerate(xs):
                spread(work, index * BLOCK, ref[...].astype(F32), ROWS)
            if decoder:
                for index, ref in enumerate(skip_wide):
                    spread(skip_work, index * BLOCK, ref[...].astype(F32), ROWS)
            for section in range(2):
                base = section * kinds
                rows = 10 - 4 * section
                start = 2 * section - 3
                ready(base)
                total = conv(work, base, rows)
                if decoder:
                    ready(base + 2)
                    total = total + conv(skip_work, base + 2, rows)
                value = finish(total, 2 * section, rows, start)
                spread(work, 0, value, rows)
                if decoder and section == 0:
                    spread(skip_work, 0, skip_narrow[...].astype(F32), 2 * ROWS)
                ready(base + 1)
                value = finish(conv(work, base + 1, rows - 2), 2 * section + 1, rows - 2, start + 1)
                if section == 0:
                    out0[...] = value.astype(BF16)
                    spread(work, 0, value, rows - 2)
                else:
                    out1[...] = value.astype(BF16)

    def call(info, xs, skips, bias, own, fetched, swapped, prev0, prev1):
        operands = [info, *xs, *skips, bias, *own, *fetched, *swapped, prev0, prev1]
        vmem = pl.BlockSpec(memory_space=pltpu.VMEM)
        far = pl.BlockSpec(memory_space=pl.ANY)
        specs = (
            [pl.BlockSpec(memory_space=pltpu.SMEM)]
            + [vmem] * (len(xs) + len(skips) + 1)
            + [far] * (3 * kinds)
            + [vmem, vmem]
        )
        scratch = [
            pltpu.VMEM((2 * kinds, TAPS, CH), BF16),
            pltpu.VMEM((3 * BLOCK, 3 * CH), BF16),
        ]
        if decoder:
            scratch.append(pltpu.VMEM((3 * BLOCK, 3 * CH), BF16))
        scratch.append(pltpu.SemaphoreType.DMA((2 * kinds, 2)))
        return pl.pallas_call(
            kernel,
            out_shape=(
                jax.ShapeDtypeStruct((2 * BLOCK, CH), BF16),
                jax.ShapeDtypeStruct((BLOCK, CH), BF16),
            ),
            in_specs=specs,
            out_specs=(vmem, vmem),
            scratch_shapes=scratch,
            compiler_params=pltpu.CompilerParams(vmem_limit_bytes=40 * 1024 * 1024),
            name="decode" if decoder else "encode",
        )(*operands)

    return call


def body(images, conv_first, conv_skip, conv_second, bias_first, bias_second):
    section = lax.axis_index("section")
    strip = lax.axis_index("strip")
    core = strip % 2
    parity = section % 2
    group = section // 2
    micro = jnp.where(group % 2 == 0, parity, 1 - parity)
    own = [w.reshape(TAPS, CH) for w in (conv_first[0], conv_second[0], conv_skip[0])]
    decoders = range(SECTIONS // 2, SECTIONS)
    cores = [(i, i ^ 1) for i in range(STRIPS)]

    def partner(block, sections=range(SECTIONS)):
        return lax.ppermute(block, "section", [(i, i ^ 1) for i in sections])

    image = lax.dynamic_index_in_dim(images, micro, 0, keepdims=False).reshape(BLOCK, CH)
    xs = (send(image, [(0, 0, 1)]), image, send(image, [(0, 0, -1)]))

    both = jnp.concatenate([bias_first, bias_second], axis=0)
    other = partner(both)
    halves = [lax.dynamic_slice_in_dim(w, core * HALF, HALF, axis=0) for w in own]
    fetched = [
        partner(halves[0]),
        partner(halves[1]),
        partner(halves[2], decoders),
    ]
    swapped = []
    for index, half in enumerate(fetched):
        if index < 2:
            swapped.append(lax.ppermute(half, "strip", cores))
        else:
            pairs = [(s * STRIPS + a, s * STRIPS + b) for s in decoders for a, b in cores]
            swapped.append(lax.ppermute(half, JOINT, pairs))
    bias = jnp.where(
        parity == 0,
        jnp.concatenate([both, other], axis=0),
        jnp.concatenate([other, both], axis=0),
    )

    def info_of(phase):
        active = (group == phase).astype(jnp.int32)
        return jnp.stack([active, parity, core, strip * ROWS]).astype(jnp.int32)

    encode = phase_kernel(False)
    decode = phase_kernel(True)
    out0 = jnp.zeros((2 * BLOCK, CH), BF16)
    out1 = jnp.zeros((BLOCK, CH), BF16)
    middle = GROUPS // 2
    for phase in range(middle):
        out0, out1 = encode(
            info_of(phase), xs, (), bias, own[:2], fetched[:2], swapped[:2], out0, out1
        )
        xs = tuple(send(out1, [(phase, phase + 1, shift)]) for shift in (1, 0, -1))
    mirror = [(g, GROUPS - 1 - g) for g in range(middle - 1)]
    narrow = send(out0, [(middle - 1, middle, 0)])
    late_wide = tuple(send(out1, [(a, b, shift) for a, b in mirror]) for shift in (1, 0, -1))
    late_narrow = send(out0, [(a, b, 0) for a, b in mirror])
    for phase in range(middle, GROUPS):
        skips = (*xs, narrow) if phase == middle else (*late_wide, late_narrow)
        out0, out1 = decode(
            info_of(phase), xs, skips, bias, own, fetched, swapped, out0, out1
        )
        if phase + 1 < GROUPS:
            xs = tuple(send(out1, [(phase, phase + 1, shift)]) for shift in (1, 0, -1))

    inner = out0[BLOCK // 2 : BLOCK // 2 + BLOCK]
    mine = jnp.where(parity == 0, inner, out1)
    theirs = partner(jnp.where(parity == 0, out1, inner))
    result = jnp.where(
        micro == 0, jnp.stack([mine, theirs]), jnp.stack([theirs, mine])
    )
    return result.reshape(1, 2, ROWS, COLS, CH)


def solution(mesh):
    placed = (
        P(None, "strip", None, None),
        P("section", None, None, None),
        P("section", None, None, None),
        P("section", None, None, None),
        P("section", None),
        P("section", None),
    )
    return jax.shard_map(
        body,
        mesh=mesh,
        in_specs=placed,
        out_specs=P("section", None, "strip", None, None),
        check_vma=False,
    )
```

```python
import jax
import jax.numpy as jnp
from jax import lax
from jax.experimental import pallas as pl
from jax.experimental.pallas import tpu as pltpu
from jax.sharding import PartitionSpec as P

BF16 = jnp.bfloat16
F32 = jnp.float32
ROWS = 4
COLS = 32
CH = 256
BLOCK = ROWS * COLS
TAPS = 9 * CH
HALF = TAPS // 2
SECTIONS = 16
STRIPS = 32
HEIGHT = ROWS * STRIPS
GROUPS = SECTIONS // 2
JOINT = ("section", "strip")


def place(group, micro):
    first = 4 * (group // 2)
    return first + (micro if group % 2 == 0 else 3 - micro)


def route(moves):
    pairs = []
    for source, target, shift in moves:
        for micro in range(2):
            for strip in range(STRIPS):
                if 0 <= strip + shift < STRIPS:
                    pairs.append(
                        (
                            place(source, micro) * STRIPS + strip,
                            place(target, micro) * STRIPS + strip + shift,
                        )
                    )
    return pairs


def send(block, moves):
    return lax.ppermute(block, JOINT, route(moves))


def phase_kernel(decoder):
    kinds = 3 if decoder else 2

    def kernel(*refs):
        refs = list(refs)
        info = refs.pop(0)
        xs = [refs.pop(0) for _ in range(3)]
        if decoder:
            skip_wide = [refs.pop(0) for _ in range(3)]
            skip_narrow = refs.pop(0)
        bias = refs.pop(0)
        weights = [refs.pop(0) for _ in range(2 * kinds)]
        prev0 = refs.pop(0)
        prev1 = refs.pop(0)
        out0 = refs.pop(0)
        out1 = refs.pop(0)
        work = refs.pop(0)
        if decoder:
            skip_work = refs.pop(0)

        active = info[0]
        top = info[1]
        @pl.when(active == 0)
        def _():
            out0[...] = prev0[...]
            out1[...] = prev1[...]

        @pl.when(active != 0)
        def _():
            def spread(dest, at, value, rows):
                size = rows * COLS
                column = lax.broadcasted_iota(jnp.int32, (size, CH), 0) & (COLS - 1)
                left = jnp.where(column == 0, 0.0, pltpu.roll(value, 1, 0))
                right = jnp.where(column == COLS - 1, 0.0, pltpu.roll(value, size - 1, 0))
                dest[at : at + size, 0:CH] = left.astype(BF16)
                dest[at : at + size, CH : 2 * CH] = value.astype(BF16)
                dest[at : at + size, 2 * CH : 3 * CH] = right.astype(BF16)

            def conv(source, slot, rows):
                size = rows * COLS
                total = None
                for tap in range(3):
                    part = jnp.dot(
                        source[tap * COLS : tap * COLS + size, :],
                        weights[slot][tap * 3 * CH : (tap + 1) * 3 * CH, :],
                        preferred_element_type=F32,
                    )
                    total = part if total is None else total + part
                return total

            def finish(total, which, rows, start):
                size = rows * COLS
                value = jnp.maximum(total + bias[which : which + 1, :], 0.0)
                row = (lax.broadcasted_iota(jnp.int32, (size, CH), 0) >> 5) + (top + start)
                value = jnp.where((row >= 0) & (row < HEIGHT), value, 0.0)
                return value.astype(BF16).astype(F32)

            for index, ref in enumerate(xs):
                spread(work, index * BLOCK, ref[...].astype(F32), ROWS)
            if decoder:
                for index, ref in enumerate(skip_wide):
                    spread(skip_work, index * BLOCK, ref[...].astype(F32), ROWS)
            for section in range(2):
                base = section * kinds
                rows = 10 - 4 * section
                start = 2 * section - 3
                total = conv(work, base, rows)
                if decoder:
                    total = total + conv(skip_work, base + 2, rows)
                value = finish(total, 2 * section, rows, start)
                spread(work, 0, value, rows)
                if decoder and section == 0:
                    spread(skip_work, 0, skip_narrow[...].astype(F32), 2 * ROWS)
                value = finish(conv(work, base + 1, rows - 2), 2 * section + 1, rows - 2, start + 1)
                if section == 0:
                    out0[...] = value.astype(BF16)
                    spread(work, 0, value, rows - 2)
                else:
                    out1[...] = value.astype(BF16)

    def call(info, xs, skips, bias, weights, prev0, prev1):
        operands = [info, *xs, *skips, bias, *weights, prev0, prev1]
        vmem = pl.BlockSpec(memory_space=pltpu.VMEM)
        specs = [pl.BlockSpec(memory_space=pltpu.SMEM)] + [vmem] * (len(operands) - 1)
        scratch = [pltpu.VMEM((3 * BLOCK, 3 * CH), BF16)]
        if decoder:
            scratch.append(pltpu.VMEM((3 * BLOCK, 3 * CH), BF16))
        return pl.pallas_call(
            kernel,
            out_shape=(
                jax.ShapeDtypeStruct((2 * BLOCK, CH), BF16),
                jax.ShapeDtypeStruct((BLOCK, CH), BF16),
            ),
            in_specs=specs,
            out_specs=(vmem, vmem),
            scratch_shapes=scratch,
            compiler_params=pltpu.CompilerParams(vmem_limit_bytes=40 * 1024 * 1024),
            name="decode" if decoder else "encode",
        )(*operands)

    return call


def body(images, conv_first, conv_skip, conv_second, bias_first, bias_second):
    section = lax.axis_index("section")
    strip = lax.axis_index("strip")
    core = strip % 2
    parity = section % 2
    group = section // 2
    micro = jnp.where(group % 2 == 0, parity, 1 - parity)
    own = [w.reshape(TAPS, CH) for w in (conv_first[0], conv_second[0], conv_skip[0])]
    decoders = range(SECTIONS // 2, SECTIONS)
    cores = [(i, i ^ 1) for i in range(STRIPS)]

    def partner(block, sections=range(SECTIONS)):
        return lax.ppermute(block, "section", [(i, i ^ 1) for i in sections])

    image = lax.dynamic_index_in_dim(images, micro, 0, keepdims=False).reshape(BLOCK, CH)
    xs = (send(image, [(0, 0, 1)]), image, send(image, [(0, 0, -1)]))

    both = jnp.concatenate([bias_first, bias_second], axis=0)
    other = partner(both)
    halves = [lax.dynamic_slice_in_dim(w, core * HALF, HALF, axis=0) for w in own]
    fetched = [
        partner(halves[0]),
        partner(halves[1]),
        partner(halves[2], decoders),
    ]
    swapped = []
    for index, half in enumerate(fetched):
        if index < 2:
            swapped.append(lax.ppermute(half, "strip", cores))
        else:
            pairs = [(s * STRIPS + a, s * STRIPS + b) for s in decoders for a, b in cores]
            swapped.append(lax.ppermute(half, JOINT, pairs))
    bias = jnp.where(
        parity == 0,
        jnp.concatenate([both, other], axis=0),
        jnp.concatenate([other, both], axis=0),
    )

    def joined(mine, half, other_half):
        remote = jnp.where(
            core == 0,
            jnp.concatenate([half, other_half], axis=0),
            jnp.concatenate([other_half, half], axis=0),
        )
        return jnp.where(parity == 0, mine, remote), jnp.where(parity == 0, remote, mine)

    by_kind = [joined(*parts) for parts in zip(own, fetched, swapped)]
    all_weights = [pair[0] for pair in by_kind] + [pair[1] for pair in by_kind]
    encode_weights = all_weights[0:2] + all_weights[3:5]

    def info_of(phase):
        active = (group == phase).astype(jnp.int32)
        return jnp.stack([active, strip * ROWS]).astype(jnp.int32)

    encode = phase_kernel(False)
    decode = phase_kernel(True)
    out0 = jnp.zeros((2 * BLOCK, CH), BF16)
    out1 = jnp.zeros((BLOCK, CH), BF16)
    middle = GROUPS // 2
    for phase in range(middle):
        out0, out1 = encode(
            info_of(phase), xs, (), bias, encode_weights, out0, out1
        )
        xs = tuple(send(out1, [(phase, phase + 1, shift)]) for shift in (1, 0, -1))
    mirror = [(g, GROUPS - 1 - g) for g in range(middle - 1)]
    narrow = send(out0, [(middle - 1, middle, 0)])
    late_wide = tuple(send(out1, [(a, b, shift) for a, b in mirror]) for shift in (1, 0, -1))
    late_narrow = send(out0, [(a, b, 0) for a, b in mirror])
    for phase in range(middle, GROUPS):
        skips = (*xs, narrow) if phase == middle else (*late_wide, late_narrow)
        out0, out1 = decode(info_of(phase), xs, skips, bias, all_weights, out0, out1)
        if phase + 1 < GROUPS:
            xs = tuple(send(out1, [(phase, phase + 1, shift)]) for shift in (1, 0, -1))

    inner = out0[BLOCK // 2 : BLOCK // 2 + BLOCK]
    mine = jnp.where(parity == 0, inner, out1)
    theirs = partner(jnp.where(parity == 0, out1, inner))
    result = jnp.where(
        micro == 0, jnp.stack([mine, theirs]), jnp.stack([theirs, mine])
    )
    return result.reshape(1, 2, ROWS, COLS, CH)


def solution(mesh):
    placed = (
        P(None, "strip", None, None),
        P("section", None, None, None),
        P("section", None, None, None),
        P("section", None, None, None),
        P("section", None),
        P("section", None),
    )
    return jax.shard_map(
        body,
        mesh=mesh,
        in_specs=placed,
        out_specs=P("section", None, "strip", None, None),
        check_vma=False,
    )
```

```python
import jax
import jax.numpy as jnp
from jax import lax
from jax.experimental import pallas as pl
from jax.experimental.pallas import tpu as pltpu
from jax.sharding import PartitionSpec as P


BF16 = jnp.bfloat16
F32 = jnp.float32
ROWS = 4
COLS = 32
CH = 256
BLOCK = ROWS * COLS
TAPS = 9 * CH
HALF = TAPS // 2
SECTIONS = 16
STRIPS = 32
HEIGHT = ROWS * STRIPS
GROUPS = SECTIONS // 2
JOINT = ("section", "strip")


def place(group, micro):
    first = 4 * (group // 2)
    return first + (micro if group % 2 == 0 else 3 - micro)


def route(moves):
    pairs = []
    for source, target, shift in moves:
        for micro in range(2):
            for strip in range(STRIPS):
                if 0 <= strip + shift < STRIPS:
                    pairs.append(
                        (
                            place(source, micro) * STRIPS + strip,
                            place(target, micro) * STRIPS + strip + shift,
                        )
                    )
    return pairs


def send(block, moves):
    return lax.ppermute(block, JOINT, route(moves))


def spread(dest, at, value, rows):
    size = rows * COLS
    column = lax.broadcasted_iota(jnp.int32, (size, CH), 0) & (COLS - 1)
    left = jnp.where(column == 0, 0.0, pltpu.roll(value, 1, 0))
    right = jnp.where(column == COLS - 1, 0.0, pltpu.roll(value, size - 1, 0))
    dest[at : at + size, 0:CH] = left.astype(BF16)
    dest[at : at + size, CH : 2 * CH] = value.astype(BF16)
    dest[at : at + size, 2 * CH : 3 * CH] = right.astype(BF16)


def conv(source, weight, rows):
    size = rows * COLS
    total = None
    for tap in range(3):
        part = jnp.dot(
            source[tap * COLS : tap * COLS + size, :],
            weight[tap * 3 * CH : (tap + 1) * 3 * CH, :],
            preferred_element_type=F32,
        )
        total = part if total is None else total + part
    return total


def finish(total, bias, rows, first, period=None):
    size = rows * COLS
    value = jnp.maximum(total + bias, 0.0)
    row = lax.broadcasted_iota(jnp.int32, (size, CH), 0) >> 5
    if period is not None:
        row = jnp.where(row < period, row, row - period)
    row = row + first
    value = jnp.where((row >= 0) & (row < HEIGHT), value, 0.0)
    return value.astype(BF16).astype(F32)


def single_kernel(halo):
    tall = ROWS + 2 * halo
    out_rows = tall - 4

    def kernel(info, *refs):
        blocks = refs[:-5]
        bias, first, second, out, work = refs[-5:]

        @pl.when(info[0] == 0)
        def _():
            out[...] = jnp.zeros(out.shape, BF16)

        @pl.when(info[0] != 0)
        def _():
            for micro in range(2):
                at = micro * tall * COLS
                for ref in blocks:
                    rows = ref.shape[1] // COLS
                    spread(work, at, ref[micro].astype(F32), rows)
                    at += rows * COLS
            top = info[1] - halo + 1
            value = finish(conv(work, first, 2 * tall - 2), bias[0:1, :], 2 * tall - 2, top, tall)
            spread(work, 0, value, 2 * tall - 2)
            value = finish(conv(work, second, 2 * tall - 4), bias[1:2, :], 2 * tall - 4, top + 1, tall)
            value = value.astype(BF16)
            for micro in range(2):
                at = micro * tall * COLS
                out[micro] = value[at : at + out_rows * COLS]

    def call(info, blocks, bias, first, second):
        vmem = pl.BlockSpec(memory_space=pltpu.VMEM)
        operands = [info, *blocks, bias, first, second]
        return pl.pallas_call(
            kernel,
            out_shape=jax.ShapeDtypeStruct((2, out_rows * COLS, CH), BF16),
            in_specs=[pl.BlockSpec(memory_space=pltpu.SMEM)] + [vmem] * (len(operands) - 1),
            out_specs=vmem,
            scratch_shapes=[pltpu.VMEM((2 * tall * COLS, 3 * CH), BF16)],
            compiler_params=pltpu.CompilerParams(vmem_limit_bytes=40 * 1024 * 1024),
        )(*operands)

    return call


def phase_kernel(decoder, doubled=False):
    kinds = 3 if decoder else 2

    def kernel(*refs):
        refs = list(refs)
        info = refs.pop(0)
        xs = [refs.pop(0) for _ in range(6 if doubled else 3)]
        if decoder:
            skip_wide = [refs.pop(0) for _ in range(3)]
            skip_narrow = refs.pop(0)
        bias = refs.pop(0)
        weights = [refs.pop(0) for _ in range(2 * kinds)]
        prev0 = refs.pop(0)
        prev1 = refs.pop(0)
        out0 = refs.pop(0)
        out1 = refs.pop(0)
        work = refs.pop(0)
        if decoder:
            skip_work = refs.pop(0)

        active = info[0]
        top = info[1]

        @pl.when(active == 0)
        def _():
            out0[...] = prev0[...]
            out1[...] = prev1[...]

        @pl.when(active != 0)
        def _():
            for index in range(3):
                value = xs[index][...].astype(F32)
                if doubled:
                    value = jnp.where(info[2] == 0, value, xs[index + 3][...].astype(F32))
                spread(work, index * BLOCK, value, ROWS)
            if decoder:
                for index, ref in enumerate(skip_wide):
                    spread(skip_work, index * BLOCK, ref[...].astype(F32), ROWS)
            for section in range(2):
                base = section * kinds
                rows = 10 - 4 * section
                start = 2 * section - 3
                total = conv(work, weights[base], rows)
                if decoder:
                    total = total + conv(skip_work, weights[base + 2], rows)
                value = finish(total, bias[2 * section : 2 * section + 1, :], rows, top + start)
                spread(work, 0, value, rows)
                if decoder and section == 0:
                    spread(skip_work, 0, skip_narrow[...].astype(F32), 2 * ROWS)
                value = finish(
                    conv(work, weights[base + 1], rows - 2),
                    bias[2 * section + 1 : 2 * section + 2, :],
                    rows - 2,
                    top + start + 1,
                )
                if section == 0:
                    out0[...] = value.astype(BF16)
                    spread(work, 0, value, rows - 2)
                else:
                    out1[...] = value.astype(BF16)

    def call(info, xs, skips, bias, weights, prev0, prev1):
        operands = [info, *xs, *skips, bias, *weights, prev0, prev1]
        vmem = pl.BlockSpec(memory_space=pltpu.VMEM)
        specs = [pl.BlockSpec(memory_space=pltpu.SMEM)] + [vmem] * (len(operands) - 1)
        scratch = [pltpu.VMEM((3 * BLOCK, 3 * CH), BF16)]
        if decoder:
            scratch.append(pltpu.VMEM((3 * BLOCK, 3 * CH), BF16))
        return pl.pallas_call(
            kernel,
            out_shape=(
                jax.ShapeDtypeStruct((2 * BLOCK, CH), BF16),
                jax.ShapeDtypeStruct((BLOCK, CH), BF16),
            ),
            in_specs=specs,
            out_specs=(vmem, vmem),
            scratch_shapes=scratch,
            compiler_params=pltpu.CompilerParams(vmem_limit_bytes=40 * 1024 * 1024),
            name="decode" if decoder else "encode",
        )(*operands)

    return call


def body(images, conv_first, conv_skip, conv_second, bias_first, bias_second):
    section = lax.axis_index("section")
    strip = lax.axis_index("strip")
    core = strip % 2
    parity = section % 2
    group = section // 2
    micro = jnp.where(group % 2 == 0, parity, 1 - parity)
    own = [w.reshape(TAPS, CH) for w in (conv_first[0], conv_second[0], conv_skip[0])]
    decoders = range(SECTIONS // 2, SECTIONS)
    pairs_from = range(2, SECTIONS)
    cores = [(i, i ^ 1) for i in range(STRIPS)]

    def shift_in_section(block, which, shift):
        return lax.ppermute(
            block,
            JOINT,
            [
                (which * STRIPS + p, which * STRIPS + p + shift)
                for p in range(STRIPS)
                if 0 <= p + shift < STRIPS
            ],
        )

    def partner(block, sections=range(SECTIONS)):
        return lax.ppermute(block, "section", [(i, i ^ 1) for i in sections])

    both = jnp.concatenate([bias_first, bias_second], axis=0)
    image = images.reshape(2, BLOCK, CH)
    below = shift_in_section(image, 0, -1)
    above = shift_in_section(image, 0, 1)
    other = partner(both, pairs_from)
    halves = [lax.dynamic_slice_in_dim(w, core * HALF, HALF, axis=0) for w in own]
    fetched = [
        partner(halves[0], pairs_from),
        partner(halves[1], pairs_from),
        partner(halves[2], decoders),
    ]

    def solo_info(which):
        active = (section == which).astype(jnp.int32)
        return jnp.stack([active, strip * ROWS]).astype(jnp.int32)

    wide = single_kernel(4)(solo_info(0), (above, image, below), both, own[0], own[1])
    handed = lax.ppermute(wide, JOINT, [(p, STRIPS + p) for p in range(STRIPS)])
    close = single_kernel(2)(solo_info(1), (handed,), both, own[0], own[1])
    xs = [None] * 6
    for shift in (1, -1, 0):
        for to in range(2):
            xs[3 * to + 1 - shift] = lax.ppermute(
                close[to],
                JOINT,
                [
                    (STRIPS + p, place(1, to) * STRIPS + p + shift)
                    for p in range(STRIPS)
                    if 0 <= p + shift < STRIPS
                ],
            )
    give = jnp.where(parity == 0, wide[1], jnp.concatenate([close[0], close[0]], axis=0))
    got = partner(give, range(2))
    level0 = jnp.where(parity == 0, wide[0], got)
    level1 = jnp.where(parity == 0, got[:BLOCK], close[1])

    swapped = [
        lax.ppermute(
            half,
            JOINT,
            [
                (s * STRIPS + a, s * STRIPS + b)
                for s in (decoders if index == 2 else pairs_from)
                for a, b in cores
            ],
        )
        for index, half in enumerate(fetched)
    ]
    bias = jnp.where(
        parity == 0,
        jnp.concatenate([both, other], axis=0),
        jnp.concatenate([other, both], axis=0),
    )

    def joined(mine, half, other_half):
        remote = jnp.where(
            core == 0,
            jnp.concatenate([half, other_half], axis=0),
            jnp.concatenate([other_half, half], axis=0),
        )
        return jnp.where(parity == 0, mine, remote), jnp.where(parity == 0, remote, mine)

    by_kind = [joined(*parts) for parts in zip(own, fetched, swapped)]
    all_weights = [pair[0] for pair in by_kind] + [pair[1] for pair in by_kind]
    encode_weights = all_weights[0:2] + all_weights[3:5]

    def info_of(phase):
        active = (group == phase).astype(jnp.int32)
        return jnp.stack([active, strip * ROWS, micro]).astype(jnp.int32)

    decode = phase_kernel(True)
    out0 = jnp.zeros((2 * BLOCK, CH), BF16)
    out1 = jnp.zeros((BLOCK, CH), BF16)
    middle = GROUPS // 2

    def onward(block, phase):
        pieces = {d: send(block, [(phase, phase + 1, d)]) for d in (1, -1, 0)}
        return (pieces[1], pieces[0], pieces[-1])

    for phase in range(1, middle):
        encode = phase_kernel(False, phase == 1)
        out0, out1 = encode(info_of(phase), xs, (), bias, encode_weights, out0, out1)
        xs = onward(out1, phase)
    mirror = [(g, GROUPS - 1 - g) for g in range(middle - 1)]
    narrow = send(out0, [(middle - 1, middle, 0)])
    out0 = jnp.where(group == 0, level0, out0)
    out1 = jnp.where(group == 0, level1, out1)
    late_wide = tuple(send(out1, [(a, b, shift) for a, b in mirror]) for shift in (1, 0, -1))
    late_narrow = send(out0, [(a, b, 0) for a, b in mirror])
    for phase in range(middle, GROUPS):
        skips = (*xs, narrow) if phase == middle else (*late_wide, late_narrow)
        out0, out1 = decode(info_of(phase), xs, skips, bias, all_weights, out0, out1)
        if phase + 1 < GROUPS:
            xs = onward(out1, phase)

    inner = out0[BLOCK // 2 : BLOCK // 2 + BLOCK]
    mine = jnp.where(parity == 0, inner, out1)
    theirs = partner(jnp.where(parity == 0, out1, inner))
    result = jnp.where(
        micro == 0, jnp.stack([mine, theirs]), jnp.stack([theirs, mine])
    )
    return result.reshape(1, 2, ROWS, COLS, CH)


def solution(mesh):
    placed = (
        P(None, "strip", None, None),
        P("section", None, None, None),
        P("section", None, None, None),
        P("section", None, None, None),
        P("section", None),
        P("section", None),
    )

    return jax.shard_map(
        body,
        mesh=mesh,
        in_specs=placed,
        out_specs=P("section", None, "strip", None, None),
        check_vma=False,
    )
```

```python
import jax
import jax.numpy as jnp
from jax import lax
from jax.experimental import pallas as pl
from jax.experimental.pallas import tpu as pltpu
from jax.sharding import PartitionSpec as P


BF16 = jnp.bfloat16
F32 = jnp.float32
ROWS = 4
COLS = 32
CH = 256
BLOCK = ROWS * COLS
TAPS = 9 * CH
HALF = TAPS // 2
SECTIONS = 16
STRIPS = 32
HEIGHT = ROWS * STRIPS
GROUPS = SECTIONS // 2
JOINT = ("section", "strip")


def place(group, micro):
    first = 4 * (group // 2)
    return first + (micro if group % 2 == 0 else 3 - micro)


def route(moves):
    pairs = []
    for source, target, shift in moves:
        for micro in range(2):
            for strip in range(STRIPS):
                if 0 <= strip + shift < STRIPS:
                    pairs.append(
                        (
                            place(source, micro) * STRIPS + strip,
                            place(target, micro) * STRIPS + strip + shift,
                        )
                    )
    return pairs


def send(block, moves):
    return lax.ppermute(block, JOINT, route(moves))


def spread(dest, at, value, rows):
    size = rows * COLS
    column = lax.broadcasted_iota(jnp.int32, (size, CH), 0) & (COLS - 1)
    left = jnp.where(column == 0, 0.0, pltpu.roll(value, 1, 0))
    right = jnp.where(column == COLS - 1, 0.0, pltpu.roll(value, size - 1, 0))
    dest[at : at + size, 0:CH] = left.astype(BF16)
    dest[at : at + size, CH : 2 * CH] = value.astype(BF16)
    dest[at : at + size, 2 * CH : 3 * CH] = right.astype(BF16)


def conv(source, weight, rows):
    size = rows * COLS
    total = None
    for tap in range(3):
        part = jnp.dot(
            source[tap * COLS : tap * COLS + size, :],
            weight[tap * 3 * CH : (tap + 1) * 3 * CH, :],
            preferred_element_type=F32,
        )
        total = part if total is None else total + part
    return total


def finish(total, bias, rows, first, period=None):
    size = rows * COLS
    value = jnp.maximum(total + bias, 0.0)
    row = lax.broadcasted_iota(jnp.int32, (size, CH), 0) >> 5
    if period is not None:
        row = jnp.where(row < period, row, row - period)
    row = row + first
    value = jnp.where((row >= 0) & (row < HEIGHT), value, 0.0)
    return value.astype(BF16).astype(F32)


def single_kernel(halo):
    tall = ROWS + 2 * halo
    out_rows = tall - 4

    def kernel(info, *refs):
        blocks = refs[:-5]
        bias, first, second, out, work = refs[-5:]

        @pl.when(info[0] == 0)
        def _():
            out[...] = jnp.zeros(out.shape, BF16)

        @pl.when(info[0] != 0)
        def _():
            for micro in range(2):
                at = micro * tall * COLS
                for ref in blocks:
                    rows = ref.shape[1] // COLS
                    spread(work, at, ref[micro].astype(F32), rows)
                    at += rows * COLS
            top = info[1] - halo + 1
            value = finish(conv(work, first, 2 * tall - 2), bias[0:1, :], 2 * tall - 2, top, tall)
            spread(work, 0, value, 2 * tall - 2)
            value = finish(conv(work, second, 2 * tall - 4), bias[1:2, :], 2 * tall - 4, top + 1, tall)
            value = value.astype(BF16)
            for micro in range(2):
                at = micro * tall * COLS
                out[micro] = value[at : at + out_rows * COLS]

    def call(info, blocks, bias, first, second):
        vmem = pl.BlockSpec(memory_space=pltpu.VMEM)
        operands = [info, *blocks, bias, first, second]
        return pl.pallas_call(
            kernel,
            out_shape=jax.ShapeDtypeStruct((2, out_rows * COLS, CH), BF16),
            in_specs=[pl.BlockSpec(memory_space=pltpu.SMEM)] + [vmem] * (len(operands) - 1),
            out_specs=vmem,
            scratch_shapes=[pltpu.VMEM((2 * tall * COLS, 3 * CH), BF16)],
            compiler_params=pltpu.CompilerParams(vmem_limit_bytes=40 * 1024 * 1024),
        )(*operands)

    return call


def phase_kernel(decoder, doubled=False, shared=False):
    kinds = 3 if decoder else 2

    def kernel(*refs):
        refs = list(refs)
        info = refs.pop(0)
        xs = [refs.pop(0) for _ in range(6 if doubled else 3)]
        if decoder:
            skips = xs if shared else [refs.pop(0) for _ in range(3)]
            skip_narrow = skips[1].at[0 : 2 * BLOCK]
            skip_wide = [skips[0], skips[1].at[2 * BLOCK : 3 * BLOCK], skips[2]]
        if shared:
            xs = skip_wide
        bias = refs.pop(0)
        weights = [refs.pop(0) for _ in range(2 * kinds)]
        prev0 = refs.pop(0)
        out0 = refs.pop(0)
        out1 = refs.pop(0)
        work = refs.pop(0)
        if decoder:
            skip_work = refs.pop(0)

        active = info[0]
        top = info[1]

        @pl.when(active == 0)
        def _():
            out0[...] = prev0[...]
            out1[...] = prev0[2 * BLOCK : 3 * BLOCK]

        @pl.when(active != 0)
        def _():
            for index in range(3):
                value = xs[index][...].astype(F32)
                if doubled:
                    value = jnp.where(info[2] == 0, value, xs[index + 3][...].astype(F32))
                spread(work, index * BLOCK, value, ROWS)
            if decoder:
                for index, ref in enumerate(skip_wide):
                    spread(skip_work, index * BLOCK, ref[...].astype(F32), ROWS)
            for section in range(2):
                base = section * kinds
                rows = 10 - 4 * section
                start = 2 * section - 3
                total = conv(work, weights[base], rows)
                if decoder:
                    total = total + conv(skip_work, weights[base + 2], rows)
                value = finish(total, bias[2 * section : 2 * section + 1, :], rows, top + start)
                spread(work, 0, value, rows)
                if decoder and section == 0:
                    spread(skip_work, 0, skip_narrow[...].astype(F32), 2 * ROWS)
                value = finish(
                    conv(work, weights[base + 1], rows - 2),
                    bias[2 * section + 1 : 2 * section + 2, :],
                    rows - 2,
                    top + start + 1,
                )
                if section == 0:
                    out0[0 : 2 * BLOCK] = value.astype(BF16)
                    spread(work, 0, value, rows - 2)
                else:
                    out0[2 * BLOCK : 3 * BLOCK] = value.astype(BF16)
                    out1[...] = value.astype(BF16)

    def call(info, xs, skips, bias, weights, prev0):
        operands = [info, *xs, *skips, bias, *weights, prev0]
        vmem = pl.BlockSpec(memory_space=pltpu.VMEM)
        specs = [pl.BlockSpec(memory_space=pltpu.SMEM)] + [vmem] * (len(operands) - 1)
        scratch = [pltpu.VMEM((3 * BLOCK, 3 * CH), BF16)]
        if decoder:
            scratch.append(pltpu.VMEM((3 * BLOCK, 3 * CH), BF16))
        return pl.pallas_call(
            kernel,
            out_shape=(
                jax.ShapeDtypeStruct((3 * BLOCK, CH), BF16),
                jax.ShapeDtypeStruct((BLOCK, CH), BF16),
            ),
            in_specs=specs,
            out_specs=(vmem, vmem),
            scratch_shapes=scratch,
            compiler_params=pltpu.CompilerParams(vmem_limit_bytes=40 * 1024 * 1024),
            name="decode" if decoder else "encode",
        )(*operands)

    return call


def body(images, conv_first, conv_skip, conv_second, bias_first, bias_second):
    section = lax.axis_index("section")
    strip = lax.axis_index("strip")
    core = strip % 2
    parity = section % 2
    group = section // 2
    micro = jnp.where(group % 2 == 0, parity, 1 - parity)
    own = [w.reshape(TAPS, CH) for w in (conv_first[0], conv_second[0], conv_skip[0])]
    decoders = range(SECTIONS // 2, SECTIONS)
    pairs_from = range(2, SECTIONS)
    cores = [(i, i ^ 1) for i in range(STRIPS)]

    def shift_in_section(block, which, shift):
        return lax.ppermute(
            block,
            JOINT,
            [
                (which * STRIPS + p, which * STRIPS + p + shift)
                for p in range(STRIPS)
                if 0 <= p + shift < STRIPS
            ],
        )

    def partner(block, sections=range(SECTIONS)):
        return lax.ppermute(block, "section", [(i, i ^ 1) for i in sections])

    both = jnp.concatenate([bias_first, bias_second], axis=0)
    image = images.reshape(2, BLOCK, CH)
    below = shift_in_section(image, 0, -1)
    above = shift_in_section(image, 0, 1)
    other = partner(both)
    halves = [lax.dynamic_slice_in_dim(w, core * HALF, HALF, axis=0) for w in own]
    fetched = [
        partner(jnp.concatenate(halves[:2], axis=0), pairs_from),
        partner(halves[2], decoders),
    ]

    def solo_info(which):
        active = (section == which).astype(jnp.int32)
        return jnp.stack([active, strip * ROWS]).astype(jnp.int32)

    wide = single_kernel(4)(solo_info(0), (above, image, below), both, own[0], own[1])
    handed = lax.ppermute(wide, JOINT, [(p, STRIPS + p) for p in range(STRIPS)])
    close = single_kernel(2)(solo_info(1), (handed,), both, own[0], own[1])
    xs = [None] * 6
    for shift in (1, -1, 0):
        for to in range(2):
            xs[3 * to + 1 - shift] = lax.ppermute(
                close[to],
                JOINT,
                [
                    (STRIPS + p, place(1, to) * STRIPS + p + shift)
                    for p in range(STRIPS)
                    if 0 <= p + shift < STRIPS
                ],
            )
    give = jnp.where(parity == 0, wide[1], jnp.concatenate([close[0], close[0]], axis=0))
    got = partner(give, range(2))
    level = jnp.where(
        parity == 0,
        jnp.concatenate([wide[0], got[:BLOCK]], axis=0),
        jnp.concatenate([got, close[1]], axis=0),
    )

    swapped = [
        lax.ppermute(
            half,
            JOINT,
            [
                (s * STRIPS + a, s * STRIPS + b)
                for s in (decoders if index == 1 else pairs_from)
                for a, b in cores
            ],
        )
        for index, half in enumerate(fetched)
    ]
    bias = jnp.where(
        parity == 0,
        jnp.concatenate([both, other], axis=0),
        jnp.concatenate([other, both], axis=0),
    )

    def joined(mine, half, other_half):
        remote = jnp.where(
            core == 0,
            jnp.concatenate([half, other_half], axis=0),
            jnp.concatenate([other_half, half], axis=0),
        )
        return jnp.where(parity == 0, mine, remote), jnp.where(parity == 0, remote, mine)

    by_kind = [
        joined(own[0], fetched[0][:HALF], swapped[0][:HALF]),
        joined(own[1], fetched[0][HALF:], swapped[0][HALF:]),
        joined(own[2], fetched[1], swapped[1]),
    ]
    all_weights = [pair[0] for pair in by_kind] + [pair[1] for pair in by_kind]
    encode_weights = all_weights[0:2] + all_weights[3:5]

    def info_of(phase):
        active = (group == phase).astype(jnp.int32)
        return jnp.stack([active, strip * ROWS, micro]).astype(jnp.int32)

    kept = jnp.zeros((3 * BLOCK, CH), BF16)
    middle = GROUPS // 2

    def onward(last, phase, centre=None):
        down = send(last, [(phase, phase + 1, 1)])
        up = send(last, [(phase, phase + 1, -1)])
        straight = send(last if centre is None else centre, [(phase, phase + 1, 0)])
        return (down, straight, up)

    for phase in range(1, middle):
        encode = phase_kernel(False, doubled=phase == 1)
        kept, last = encode(info_of(phase), xs, (), bias, encode_weights, kept)
        xs = onward(last, phase, kept if phase + 1 == middle else None)
    mirror = [(g, GROUPS - 1 - g) for g in range(middle - 1)]
    kept = jnp.where(group == 0, level, kept)
    last = jnp.where(group == 0, level[2 * BLOCK :], last)
    late = tuple(
        send(kept if shift == 0 else last, [(a, b, shift) for a, b in mirror])
        for shift in (1, 0, -1)
    )
    for phase in range(middle, GROUPS):
        shared = phase == middle
        decode = phase_kernel(True, shared=shared)
        kept, last = decode(
            info_of(phase), xs, () if shared else late, bias, all_weights, kept
        )
        if phase + 1 < GROUPS:
            xs = onward(last, phase)

    inner = kept[BLOCK // 2 : BLOCK // 2 + BLOCK]
    mine = jnp.where(parity == 0, inner, last)
    theirs = partner(jnp.where(parity == 0, last, inner))
    result = jnp.where(
        micro == 0, jnp.stack([mine, theirs]), jnp.stack([theirs, mine])
    )
    return result.reshape(1, 2, ROWS, COLS, CH)


def solution(mesh):
    placed = (
        P(None, "strip", None, None),
        P("section", None, None, None),
        P("section", None, None, None),
        P("section", None, None, None),
        P("section", None),
        P("section", None),
    )

    return jax.shard_map(
        body,
        mesh=mesh,
        in_specs=placed,
        out_specs=P("section", None, "strip", None, None),
        check_vma=False,
    )
```

```python
import jax
import jax.numpy as jnp
from jax import lax
from jax.experimental import pallas as pl
from jax.experimental.pallas import tpu as pltpu
from jax.sharding import PartitionSpec as P


BF16 = jnp.bfloat16
F32 = jnp.float32
ROWS = 4
COLS = 32
CH = 256
BLOCK = ROWS * COLS
TAPS = 9 * CH
HALF = TAPS // 2
SECTIONS = 16
STRIPS = 32
HEIGHT = ROWS * STRIPS
GROUPS = SECTIONS // 2
JOINT = ("section", "strip")


def place(group, micro):
    first = 4 * (group // 2)
    return first + (micro if group % 2 == 0 else 3 - micro)


def route(moves):
    pairs = []
    for source, target, shift in moves:
        for micro in range(2):
            for strip in range(STRIPS):
                if 0 <= strip + shift < STRIPS:
                    pairs.append(
                        (
                            place(source, micro) * STRIPS + strip,
                            place(target, micro) * STRIPS + strip + shift,
                        )
                    )
    return pairs


def send(block, moves):
    return lax.ppermute(block, JOINT, route(moves))


def spread(dest, at, value, rows):
    size = rows * COLS
    column = lax.broadcasted_iota(jnp.int32, (size, CH), 0) & (COLS - 1)
    left = jnp.where(column == 0, 0.0, pltpu.roll(value, 1, 0))
    right = jnp.where(column == COLS - 1, 0.0, pltpu.roll(value, size - 1, 0))
    dest[at : at + size, 0:CH] = left.astype(BF16)
    dest[at : at + size, CH : 2 * CH] = value.astype(BF16)
    dest[at : at + size, 2 * CH : 3 * CH] = right.astype(BF16)


def conv(source, weight, rows):
    size = rows * COLS
    total = None
    for tap in range(3):
        part = jnp.dot(
            source[tap * COLS : tap * COLS + size, :],
            weight[tap * 3 * CH : (tap + 1) * 3 * CH, :],
            preferred_element_type=F32,
        )
        total = part if total is None else total + part
    return total


def finish(total, bias, rows, first, period=None):
    size = rows * COLS
    value = jnp.maximum(total + bias, 0.0)
    row = lax.broadcasted_iota(jnp.int32, (size, CH), 0) >> 5
    if period is not None:
        row = jnp.where(row < period, row, row - period)
    row = row + first
    value = jnp.where((row >= 0) & (row < HEIGHT), value, 0.0)
    return value.astype(BF16).astype(F32)


def single_kernel(halo):
    tall = ROWS + 2 * halo
    out_rows = tall - 4

    def kernel(info, *refs):
        blocks = refs[:-5]
        bias, first, second, out, work = refs[-5:]

        @pl.when(info[0] == 0)
        def _():
            out[...] = jnp.zeros(out.shape, BF16)

        @pl.when(info[0] != 0)
        def _():
            for micro in range(2):
                at = micro * tall * COLS
                for ref in blocks:
                    rows = ref.shape[1] // COLS
                    spread(work, at, ref[micro].astype(F32), rows)
                    at += rows * COLS
            top = info[1] - halo + 1
            value = finish(conv(work, first, 2 * tall - 2), bias[0:1, :], 2 * tall - 2, top, tall)
            spread(work, 0, value, 2 * tall - 2)
            value = finish(conv(work, second, 2 * tall - 4), bias[1:2, :], 2 * tall - 4, top + 1, tall)
            value = value.astype(BF16)
            for micro in range(2):
                at = micro * tall * COLS
                out[micro] = value[at : at + out_rows * COLS]

    def call(info, blocks, bias, first, second):
        vmem = pl.BlockSpec(memory_space=pltpu.VMEM)
        operands = [info, *blocks, bias, first, second]
        return pl.pallas_call(
            kernel,
            out_shape=jax.ShapeDtypeStruct((2, out_rows * COLS, CH), BF16),
            in_specs=[pl.BlockSpec(memory_space=pltpu.SMEM)] + [vmem] * (len(operands) - 1),
            out_specs=vmem,
            scratch_shapes=[pltpu.VMEM((2 * tall * COLS, 3 * CH), BF16)],
            compiler_params=pltpu.CompilerParams(vmem_limit_bytes=40 * 1024 * 1024),
        )(*operands)

    return call


def phase_kernel(decoder, doubled=False, mated=False, shared=False):
    kinds = 3 if decoder else 2

    def kernel(*refs):
        refs = list(refs)
        info = refs.pop(0)
        xs = [refs.pop(0) for _ in range(6 if doubled else 3)]
        if mated:
            straight, mate, far = xs
            if shared:
                mate = mate.at[2 * BLOCK : 3 * BLOCK]
            own_rows = straight.at[2 * BLOCK : 3 * BLOCK] if shared else straight
        if decoder:
            if shared:
                skip_narrow = straight.at[0 : 2 * BLOCK]
            else:
                skips = [refs.pop(0) for _ in range(3)]
                skip_narrow = skips[1].at[0 : 2 * BLOCK]
                skip_wide = [skips[0], skips[1].at[2 * BLOCK : 3 * BLOCK], skips[2]]
        bias = refs.pop(0)
        weights = [refs.pop(0) for _ in range(2 * kinds)]
        prev0 = refs.pop(0)
        out0 = refs.pop(0)
        out1 = refs.pop(0)
        work = refs.pop(0)
        if decoder:
            skip_work = refs.pop(0)

        active = info[0]
        top = info[1]

        @pl.when(active == 0)
        def _():
            out0[...] = prev0[...]
            out1[...] = prev0[2 * BLOCK : 3 * BLOCK]

        @pl.when(active != 0)
        def _():
            def piece(index):
                if mated:
                    if index == 1:
                        return own_rows[...].astype(F32)
                    sides = (far, mate) if index == 0 else (mate, far)
                    return jnp.where(
                        info[3] == 0, sides[0][...].astype(F32), sides[1][...].astype(F32)
                    )
                value = xs[index][...].astype(F32)
                if doubled:
                    value = jnp.where(info[2] == 0, value, xs[index + 3][...].astype(F32))
                return value

            for index in range(3):
                value = piece(index)
                spread(work, index * BLOCK, value, ROWS)
                if shared:
                    spread(skip_work, index * BLOCK, value, ROWS)
            if decoder and not shared:
                for index, ref in enumerate(skip_wide):
                    spread(skip_work, index * BLOCK, ref[...].astype(F32), ROWS)
            for section in range(2):
                base = section * kinds
                rows = 10 - 4 * section
                start = 2 * section - 3
                total = conv(work, weights[base], rows)
                if decoder:
                    total = total + conv(skip_work, weights[base + 2], rows)
                value = finish(total, bias[2 * section : 2 * section + 1, :], rows, top + start)
                spread(work, 0, value, rows)
                if decoder and section == 0:
                    spread(skip_work, 0, skip_narrow[...].astype(F32), 2 * ROWS)
                value = finish(
                    conv(work, weights[base + 1], rows - 2),
                    bias[2 * section + 1 : 2 * section + 2, :],
                    rows - 2,
                    top + start + 1,
                )
                if section == 0:
                    out0[0 : 2 * BLOCK] = value.astype(BF16)
                    spread(work, 0, value, rows - 2)
                else:
                    out0[2 * BLOCK : 3 * BLOCK] = value.astype(BF16)
                    out1[...] = value.astype(BF16)

    def call(info, xs, skips, bias, weights, prev0):
        operands = [info, *xs, *skips, bias, *weights, prev0]
        vmem = pl.BlockSpec(memory_space=pltpu.VMEM)
        specs = [pl.BlockSpec(memory_space=pltpu.SMEM)] + [vmem] * (len(operands) - 1)
        scratch = [pltpu.VMEM((3 * BLOCK, 3 * CH), BF16)]
        if decoder:
            scratch.append(pltpu.VMEM((3 * BLOCK, 3 * CH), BF16))
        return pl.pallas_call(
            kernel,
            out_shape=(
                jax.ShapeDtypeStruct((3 * BLOCK, CH), BF16),
                jax.ShapeDtypeStruct((BLOCK, CH), BF16),
            ),
            in_specs=specs,
            out_specs=(vmem, vmem),
            scratch_shapes=scratch,
            compiler_params=pltpu.CompilerParams(vmem_limit_bytes=40 * 1024 * 1024),
            name="decode" if decoder else "encode",
        )(*operands)

    return call


def body(images, conv_first, conv_skip, conv_second, bias_first, bias_second):
    section = lax.axis_index("section")
    strip = lax.axis_index("strip")
    core = strip % 2
    parity = section % 2
    group = section // 2
    micro = jnp.where(group % 2 == 0, parity, 1 - parity)
    own = [w.reshape(TAPS, CH) for w in (conv_first[0], conv_second[0], conv_skip[0])]
    decoders = range(SECTIONS // 2, SECTIONS)
    pairs_from = range(2, SECTIONS)
    cores = [(i, i ^ 1) for i in range(STRIPS)]

    def shift_in_section(block, which, shift):
        return lax.ppermute(
            block,
            JOINT,
            [
                (which * STRIPS + p, which * STRIPS + p + shift)
                for p in range(STRIPS)
                if 0 <= p + shift < STRIPS
            ],
        )

    def partner(block, sections=range(SECTIONS)):
        return lax.ppermute(block, "section", [(i, i ^ 1) for i in sections])

    both = jnp.concatenate([bias_first, bias_second], axis=0)
    image = images.reshape(2, BLOCK, CH)
    below = shift_in_section(image, 0, -1)
    above = shift_in_section(image, 0, 1)
    fetched = [
        partner(jnp.where(core == 0, own[0], own[1]), pairs_from),
        partner(lax.dynamic_slice_in_dim(own[2], core * HALF, HALF, axis=0), decoders),
    ]

    def solo_info(which):
        active = (section == which).astype(jnp.int32)
        return jnp.stack([active, strip * ROWS]).astype(jnp.int32)

    wide = single_kernel(4)(solo_info(0), (above, image, below), both, own[0], own[1])
    handed = lax.ppermute(wide, JOINT, [(p, STRIPS + p) for p in range(STRIPS)])
    close = single_kernel(2)(solo_info(1), (handed,), both, own[0], own[1])
    xs = [None] * 6
    for shift in (1, -1, 0):
        for to in range(2):
            xs[3 * to + 1 - shift] = lax.ppermute(
                close[to],
                JOINT,
                [
                    (STRIPS + p, place(1, to) * STRIPS + p + shift)
                    for p in range(STRIPS)
                    if 0 <= p + shift < STRIPS
                ],
            )
    other = partner(both)
    give = jnp.where(parity == 0, wide[1], jnp.concatenate([close[0], close[0]], axis=0))
    got = partner(give, range(2))
    level = jnp.where(
        parity == 0,
        jnp.concatenate([wide[0], got[:BLOCK]], axis=0),
        jnp.concatenate([got, close[1]], axis=0),
    )

    swapped = [
        lax.ppermute(
            half,
            JOINT,
            [
                (s * STRIPS + a, s * STRIPS + b)
                for s in (decoders if index == 1 else pairs_from)
                for a, b in cores
            ],
        )
        for index, half in enumerate(fetched)
    ]
    bias = jnp.where(
        parity == 0,
        jnp.concatenate([both, other], axis=0),
        jnp.concatenate([other, both], axis=0),
    )

    def in_order(mine, remote):
        return jnp.where(parity == 0, mine, remote), jnp.where(parity == 0, remote, mine)

    def by_core(at_zero, at_one):
        return jnp.where(core == 0, at_zero, at_one)

    skip_halves = jnp.where(
        core == 0,
        jnp.concatenate([fetched[1], swapped[1]], axis=0),
        jnp.concatenate([swapped[1], fetched[1]], axis=0),
    )
    by_kind = [
        in_order(own[0], by_core(fetched[0], swapped[0])),
        in_order(own[1], by_core(swapped[0], fetched[0])),
        in_order(own[2], skip_halves),
    ]
    all_weights = [pair[0] for pair in by_kind] + [pair[1] for pair in by_kind]
    encode_weights = all_weights[0:2] + all_weights[3:5]

    def info_of(phase):
        active = (group == phase).astype(jnp.int32)
        return jnp.stack([active, strip * ROWS, micro, core]).astype(jnp.int32)

    kept = jnp.zeros((3 * BLOCK, CH), BF16)
    middle = GROUPS // 2

    def onward(last, phase, centre=None):
        following = phase + 1
        if phase % 2:
            straight = send(last if centre is None else centre, [(phase, following, 0)])
            far = lax.ppermute(
                last,
                JOINT,
                [
                    (
                        place(phase, m) * STRIPS + p + (1 if p % 2 else -1),
                        place(following, m) * STRIPS + p,
                    )
                    for m in range(2)
                    for p in range(1, STRIPS - 1)
                ],
            )
        else:
            down = send(last, [(phase, following, 1)])
            up = send(last, [(phase, following, -1)])
            return (down, send(last, [(phase, following, 0)]), up)
        mate = lax.ppermute(
            straight,
            JOINT,
            [
                (place(following, m) * STRIPS + a, place(following, m) * STRIPS + b)
                for m in range(2)
                for a, b in cores
            ],
        )
        return (straight, mate, far)

    for phase in range(1, middle):
        encode = phase_kernel(False, doubled=phase == 1, mated=phase % 2 == 0)
        kept, last = encode(info_of(phase), xs, (), bias, encode_weights, kept)
        xs = onward(last, phase, kept if phase + 1 == middle else None)
    mirror = [(g, GROUPS - 1 - g) for g in range(middle - 1)]
    kept = jnp.where(group == 0, level, kept)
    last = jnp.where(group == 0, level[2 * BLOCK :], last)
    late = tuple(
        send(kept if shift == 0 else last, [(a, b, shift) for a, b in mirror])
        for shift in (1, 0, -1)
    )
    for phase in range(middle, GROUPS):
        shared = phase == middle
        decode = phase_kernel(True, mated=phase % 2 == 0, shared=shared)
        kept, last = decode(
            info_of(phase), xs, () if shared else late, bias, all_weights, kept
        )
        if phase + 1 < GROUPS:
            xs = onward(last, phase)

    inner = kept[BLOCK // 2 : BLOCK // 2 + BLOCK]
    mine = jnp.where(parity == 0, inner, last)
    theirs = partner(jnp.where(parity == 0, last, inner))
    result = jnp.where(
        micro == 0, jnp.stack([mine, theirs]), jnp.stack([theirs, mine])
    )
    return result.reshape(1, 2, ROWS, COLS, CH)


def solution(mesh):
    placed = (
        P(None, "strip", None, None),
        P("section", None, None, None),
        P("section", None, None, None),
        P("section", None, None, None),
        P("section", None),
        P("section", None),
    )

    return jax.shard_map(
        body,
        mesh=mesh,
        in_specs=placed,
        out_specs=P("section", None, "strip", None, None),
        check_vma=False,
    )
```

```python
import jax
import jax.numpy as jnp
from jax import lax
from jax.experimental import pallas as pl
from jax.experimental.pallas import tpu as pltpu
from jax.sharding import PartitionSpec as P


BF16 = jnp.bfloat16
F32 = jnp.float32
ROWS = 4
COLS = 32
CH = 256
BLOCK = ROWS * COLS
TAPS = 9 * CH
HALF = TAPS // 2
SECTIONS = 16
STRIPS = 32
HEIGHT = ROWS * STRIPS
GROUPS = SECTIONS // 2
JOINT = ("section", "strip")
VMEM_LIMIT = 16 * 1024 * 1024


def place(group, micro):
    first = 4 * (group // 2)
    return first + (micro if group % 2 == 0 else 3 - micro)


def route(moves):
    pairs = []
    for source, target, shift in moves:
        for micro in range(2):
            for strip in range(STRIPS):
                if 0 <= strip + shift < STRIPS:
                    pairs.append(
                        (
                            place(source, micro) * STRIPS + strip,
                            place(target, micro) * STRIPS + strip + shift,
                        )
                    )
    return pairs


def send(block, moves):
    return lax.ppermute(block, JOINT, route(moves))


def spread(dest, at, value, rows):
    size = rows * COLS
    column = lax.broadcasted_iota(jnp.int32, (size, CH), 0) & (COLS - 1)
    left = jnp.where(column == 0, 0.0, pltpu.roll(value, 1, 0))
    right = jnp.where(column == COLS - 1, 0.0, pltpu.roll(value, size - 1, 0))
    dest[at : at + size, 0:CH] = left.astype(BF16)
    dest[at : at + size, CH : 2 * CH] = value.astype(BF16)
    dest[at : at + size, 2 * CH : 3 * CH] = right.astype(BF16)


def conv(source, weight, rows):
    size = rows * COLS
    total = None
    for tap in range(3):
        part = jnp.dot(
            source[tap * COLS : tap * COLS + size, :],
            weight[tap * 3 * CH : (tap + 1) * 3 * CH, :],
            preferred_element_type=F32,
        )
        total = part if total is None else total + part
    return total


def finish(total, bias, rows, first, period=None):
    size = rows * COLS
    value = jnp.maximum(total + bias, 0.0)
    row = lax.broadcasted_iota(jnp.int32, (size, CH), 0) >> 5
    if period is not None:
        row = jnp.where(row < period, row, row - period)
    row = row + first
    value = jnp.where((row >= 0) & (row < HEIGHT), value, 0.0)
    return value.astype(BF16).astype(F32)


def single_kernel(which, halo):
    tall = ROWS + 2 * halo
    out_rows = tall - 4

    def kernel(info, *refs):
        blocks = refs[:-5]
        bias, first, second, out, work = refs[-5:]

        @pl.when(info[4] != which)
        def _():
            out[...] = jnp.zeros(out.shape, BF16)

        @pl.when(info[4] == which)
        def _():
            for micro in range(2):
                at = micro * tall * COLS
                for ref in blocks:
                    rows = ref.shape[1] // COLS
                    spread(work, at, ref[micro].astype(F32), rows)
                    at += rows * COLS
            top = info[1] - halo + 1
            value = finish(conv(work, first, 2 * tall - 2), bias[0:1, :], 2 * tall - 2, top, tall)
            spread(work, 0, value, 2 * tall - 2)
            value = finish(conv(work, second, 2 * tall - 4), bias[1:2, :], 2 * tall - 4, top + 1, tall)
            value = value.astype(BF16)
            for micro in range(2):
                at = micro * tall * COLS
                out[micro] = value[at : at + out_rows * COLS]

    def call(info, blocks, bias, first, second):
        vmem = pl.BlockSpec(memory_space=pltpu.VMEM)
        operands = [info, *blocks, bias, first, second]
        return pl.pallas_call(
            kernel,
            out_shape=jax.ShapeDtypeStruct((2, out_rows * COLS, CH), BF16),
            in_specs=[pl.BlockSpec(memory_space=pltpu.SMEM)] + [vmem] * (len(operands) - 1),
            out_specs=vmem,
            scratch_shapes=[pltpu.VMEM((2 * tall * COLS, 3 * CH), BF16)],
            compiler_params=pltpu.CompilerParams(vmem_limit_bytes=VMEM_LIMIT),
        )(*operands)

    return call


def phase_kernel(phase, decoder, doubled=False, mated=False, shared=False):
    kinds = 3 if decoder else 2

    def kernel(*refs):
        refs = list(refs)
        info = refs.pop(0)
        xs = [refs.pop(0) for _ in range(6 if doubled else 3)]
        if mated:
            straight, mate, far = xs
            if shared:
                mate = mate.at[2 * BLOCK : 3 * BLOCK]
            own_rows = straight.at[2 * BLOCK : 3 * BLOCK] if shared else straight
        if decoder:
            if shared:
                skip_narrow = straight.at[0 : 2 * BLOCK]
            else:
                skips = [refs.pop(0) for _ in range(3)]
                skip_narrow = skips[1].at[0 : 2 * BLOCK]
                skip_wide = [skips[0], skips[1].at[2 * BLOCK : 3 * BLOCK], skips[2]]
        bias = refs.pop(0)
        weights = [refs.pop(0) for _ in range(2 * kinds)]
        prev0 = refs.pop(0)
        out0 = refs.pop(0)
        out1 = refs.pop(0)
        work = refs.pop(0)
        if decoder:
            skip_work = refs.pop(0)

        active = (info[0] == phase).astype(jnp.int32)
        top = info[1]

        @pl.when(active == 0)
        def _():
            out0[...] = prev0[...]
            out1[...] = prev0[2 * BLOCK : 3 * BLOCK]

        @pl.when(active != 0)
        def _():
            def piece(index):
                if mated:
                    if index == 1:
                        return own_rows[...].astype(F32)
                    sides = (far, mate) if index == 0 else (mate, far)
                    return jnp.where(
                        info[3] == 0, sides[0][...].astype(F32), sides[1][...].astype(F32)
                    )
                value = xs[index][...].astype(F32)
                if doubled:
                    value = jnp.where(info[2] == 0, value, xs[index + 3][...].astype(F32))
                return value

            for index in range(3):
                value = piece(index)
                spread(work, index * BLOCK, value, ROWS)
                if shared:
                    spread(skip_work, index * BLOCK, value, ROWS)
            if decoder and not shared:
                for index, ref in enumerate(skip_wide):
                    spread(skip_work, index * BLOCK, ref[...].astype(F32), ROWS)
            for section in range(2):
                base = section * kinds
                rows = 10 - 4 * section
                start = 2 * section - 3
                total = conv(work, weights[base], rows)
                if decoder:
                    total = total + conv(skip_work, weights[base + 2], rows)
                value = finish(total, bias[2 * section : 2 * section + 1, :], rows, top + start)
                spread(work, 0, value, rows)
                if decoder and section == 0:
                    spread(skip_work, 0, skip_narrow[...].astype(F32), 2 * ROWS)
                value = finish(
                    conv(work, weights[base + 1], rows - 2),
                    bias[2 * section + 1 : 2 * section + 2, :],
                    rows - 2,
                    top + start + 1,
                )
                if section == 0:
                    out0[0 : 2 * BLOCK] = value.astype(BF16)
                    spread(work, 0, value, rows - 2)
                else:
                    out0[2 * BLOCK : 3 * BLOCK] = value.astype(BF16)
                    out1[...] = value.astype(BF16)

    def call(info, xs, skips, bias, weights, prev0):
        operands = [info, *xs, *skips, bias, *weights, prev0]
        vmem = pl.BlockSpec(memory_space=pltpu.VMEM)
        specs = [pl.BlockSpec(memory_space=pltpu.SMEM)] + [vmem] * (len(operands) - 1)
        scratch = [pltpu.VMEM((3 * BLOCK, 3 * CH), BF16)]
        if decoder:
            scratch.append(pltpu.VMEM((3 * BLOCK, 3 * CH), BF16))
        return pl.pallas_call(
            kernel,
            out_shape=(
                jax.ShapeDtypeStruct((3 * BLOCK, CH), BF16),
                jax.ShapeDtypeStruct((BLOCK, CH), BF16),
            ),
            in_specs=specs,
            out_specs=(vmem, vmem),
            scratch_shapes=scratch,
            compiler_params=pltpu.CompilerParams(vmem_limit_bytes=VMEM_LIMIT),
            name="decode" if decoder else "encode",
        )(*operands)

    return call


def body(images, conv_first, conv_skip, conv_second, bias_first, bias_second):
    section = lax.axis_index("section")
    strip = lax.axis_index("strip")
    core = strip % 2
    parity = section % 2
    group = section // 2
    micro = jnp.where(group % 2 == 0, parity, 1 - parity)
    info = jnp.stack([group, strip * ROWS, micro, core, section]).astype(jnp.int32)
    images, info, core_zero, even, group_zero, micro_zero = lax.optimization_barrier(
        (images, info, core == 0, parity == 0, group == 0, micro == 0)
    )
    own = [w.reshape(TAPS, CH) for w in (conv_first[0], conv_second[0], conv_skip[0])]
    decoders = range(SECTIONS // 2, SECTIONS)
    pairs_from = range(2, SECTIONS)
    cores = [(i, i ^ 1) for i in range(STRIPS)]

    def shift_in_section(block, which, shift):
        return lax.ppermute(
            block,
            JOINT,
            [
                (which * STRIPS + p, which * STRIPS + p + shift)
                for p in range(STRIPS)
                if 0 <= p + shift < STRIPS
            ],
        )

    def partner(block, sections=range(SECTIONS)):
        return lax.ppermute(block, "section", [(i, i ^ 1) for i in sections])

    both = jnp.concatenate([bias_first, bias_second], axis=0)
    image = images.reshape(2, BLOCK, CH)
    below = shift_in_section(image, 0, -1)
    above = shift_in_section(image, 0, 1)
    fetched = [
        partner(jnp.where(core_zero, own[0], own[1]), pairs_from),
        partner(lax.dynamic_slice_in_dim(own[2], core * HALF, HALF, axis=0), decoders),
    ]

    wide = single_kernel(0, 4)(info, (above, image, below), both, own[0], own[1])
    handed = lax.ppermute(wide, JOINT, [(p, STRIPS + p) for p in range(STRIPS)])
    close = single_kernel(1, 2)(info, (handed,), both, own[0], own[1])
    xs = [None] * 6
    for shift in (1, -1, 0):
        for to in range(2):
            xs[3 * to + 1 - shift] = lax.ppermute(
                close[to],
                JOINT,
                [
                    (STRIPS + p, place(1, to) * STRIPS + p + shift)
                    for p in range(STRIPS)
                    if 0 <= p + shift < STRIPS
                ],
            )
    other = partner(both)
    give = jnp.where(even, wide[1], jnp.concatenate([close[0], close[0]], axis=0))
    got = partner(give, range(2))
    level = jnp.where(
        even,
        jnp.concatenate([wide[0], got[:BLOCK]], axis=0),
        jnp.concatenate([got, close[1]], axis=0),
    )

    swapped = [
        lax.ppermute(
            half,
            JOINT,
            [
                (s * STRIPS + a, s * STRIPS + b)
                for s in (decoders if index == 1 else pairs_from)
                for a, b in cores
            ],
        )
        for index, half in enumerate(fetched)
    ]
    bias = jnp.where(
        even,
        jnp.concatenate([both, other], axis=0),
        jnp.concatenate([other, both], axis=0),
    )

    def in_order(mine, remote):
        return jnp.where(even, mine, remote), jnp.where(even, remote, mine)

    def by_core(at_zero, at_one):
        return jnp.where(core_zero, at_zero, at_one)

    skip_halves = jnp.where(
        core_zero,
        jnp.concatenate([fetched[1], swapped[1]], axis=0),
        jnp.concatenate([swapped[1], fetched[1]], axis=0),
    )
    by_kind = [
        in_order(own[0], by_core(fetched[0], swapped[0])),
        in_order(own[1], by_core(swapped[0], fetched[0])),
        in_order(own[2], skip_halves),
    ]
    all_weights = [pair[0] for pair in by_kind] + [pair[1] for pair in by_kind]
    encode_weights = all_weights[0:2] + all_weights[3:5]

    kept = jnp.zeros((3 * BLOCK, CH), BF16)
    middle = GROUPS // 2

    def onward(last, phase, centre=None):
        following = phase + 1
        if phase % 2:
            straight = send(last if centre is None else centre, [(phase, following, 0)])
            far = lax.ppermute(
                last,
                JOINT,
                [
                    (
                        place(phase, m) * STRIPS + p + (1 if p % 2 else -1),
                        place(following, m) * STRIPS + p,
                    )
                    for m in range(2)
                    for p in range(1, STRIPS - 1)
                ],
            )
        else:
            down = send(last, [(phase, following, 1)])
            up = send(last, [(phase, following, -1)])
            return (down, send(last, [(phase, following, 0)]), up)
        mate = lax.ppermute(
            straight,
            JOINT,
            [
                (place(following, m) * STRIPS + a, place(following, m) * STRIPS + b)
                for m in range(2)
                for a, b in cores
            ],
        )
        return (straight, mate, far)

    for phase in range(1, middle):
        encode = phase_kernel(phase, False, doubled=phase == 1, mated=phase % 2 == 0)
        kept, last = encode(info, xs, (), bias, encode_weights, kept)
        xs = onward(last, phase, kept if phase + 1 == middle else None)
    mirror = [(g, GROUPS - 1 - g) for g in range(middle - 1)]
    kept = jnp.where(group_zero, level, kept)
    last = jnp.where(group_zero, level[2 * BLOCK :], last)
    late = tuple(
        send(kept if shift == 0 else last, [(a, b, shift) for a, b in mirror])
        for shift in (1, 0, -1)
    )
    for phase in range(middle, GROUPS):
        shared = phase == middle
        decode = phase_kernel(phase, True, mated=phase % 2 == 0, shared=shared)
        kept, last = decode(
            info, xs, () if shared else late, bias, all_weights, kept
        )
        if phase + 1 < GROUPS:
            xs = onward(last, phase)

    inner = kept[BLOCK // 2 : BLOCK // 2 + BLOCK]
    mine = jnp.where(even, inner, last)
    theirs = partner(jnp.where(even, last, inner))
    result = jnp.where(
        micro_zero, jnp.stack([mine, theirs]), jnp.stack([theirs, mine])
    )
    return result.reshape(1, 2, ROWS, COLS, CH)


def solution(mesh):
    placed = (
        P(None, "strip", None, None),
        P("section", None, None, None),
        P("section", None, None, None),
        P("section", None, None, None),
        P("section", None),
        P("section", None),
    )

    return jax.shard_map(
        body,
        mesh=mesh,
        in_specs=placed,
        out_specs=P("section", None, "strip", None, None),
        check_vma=False,
    )
```

```python
import jax
import jax.numpy as jnp
from jax import lax
from jax.experimental import pallas as pl
from jax.experimental.pallas import tpu as pltpu
from jax.sharding import PartitionSpec as P


BF16 = jnp.bfloat16
F32 = jnp.float32
ROWS = 4
COLS = 32
CH = 256
BLOCK = ROWS * COLS
TAPS = 9 * CH
SECTIONS = 16
STRIPS = 32
HEIGHT = ROWS * STRIPS
GROUPS = SECTIONS // 2
JOINT = ("section", "strip")
VMEM_LIMIT = 16 * 1024 * 1024


def place(group, micro):
    first = 4 * (group // 2)
    return first + (micro if group % 2 == 0 else 3 - micro)


def route(moves):
    pairs = []
    for source, target, shift in moves:
        for micro in range(2):
            for strip in range(STRIPS):
                if 0 <= strip + shift < STRIPS:
                    pairs.append(
                        (
                            place(source, micro) * STRIPS + strip,
                            place(target, micro) * STRIPS + strip + shift,
                        )
                    )
    return pairs


def send(block, moves):
    return lax.ppermute(block, JOINT, route(moves))


def spread(dest, at, value, rows):
    size = rows * COLS
    column = lax.broadcasted_iota(jnp.int32, (size, CH), 0) & (COLS - 1)
    left = jnp.where(column == 0, 0.0, pltpu.roll(value, 1, 0))
    right = jnp.where(column == COLS - 1, 0.0, pltpu.roll(value, size - 1, 0))
    dest[at : at + size, 0:CH] = left.astype(BF16)
    dest[at : at + size, CH : 2 * CH] = value.astype(BF16)
    dest[at : at + size, 2 * CH : 3 * CH] = right.astype(BF16)


def conv(source, weight, rows):
    size = rows * COLS
    total = None
    for tap in range(3):
        part = jnp.dot(
            source[tap * COLS : tap * COLS + size, :],
            weight[tap * 3 * CH : (tap + 1) * 3 * CH, :],
            preferred_element_type=F32,
        )
        total = part if total is None else total + part
    return total


def finish(total, bias, rows, first, period=None):
    size = rows * COLS
    value = jnp.maximum(total + bias, 0.0)
    row = lax.broadcasted_iota(jnp.int32, (size, CH), 0) >> 5
    if period is not None:
        row = jnp.where(row < period, row, row - period)
    row = row + first
    value = jnp.where((row >= 0) & (row < HEIGHT), value, 0.0)
    return value.astype(BF16).astype(F32)


def single_kernel(which, halo):
    tall = ROWS + 2 * halo
    out_rows = tall - 4

    def kernel(info, *refs):
        blocks = refs[:-5]
        bias, first, second, out, work = refs[-5:]

        @pl.when(info[4] != which)
        def _():
            out[...] = jnp.zeros(out.shape, BF16)

        @pl.when(info[4] == which)
        def _():
            for micro in range(2):
                at = micro * tall * COLS
                for ref in blocks:
                    rows = ref.shape[1] // COLS
                    spread(work, at, ref[micro].astype(F32), rows)
                    at += rows * COLS
            top = info[1] - halo + 1
            value = finish(conv(work, first, 2 * tall - 2), bias[0:1, :], 2 * tall - 2, top, tall)
            spread(work, 0, value, 2 * tall - 2)
            value = finish(conv(work, second, 2 * tall - 4), bias[1:2, :], 2 * tall - 4, top + 1, tall)
            value = value.astype(BF16)
            for micro in range(2):
                at = micro * tall * COLS
                out[micro] = value[at : at + out_rows * COLS]

    def call(info, blocks, bias, first, second):
        vmem = pl.BlockSpec(memory_space=pltpu.VMEM)
        operands = [info, *blocks, bias, first, second]
        return pl.pallas_call(
            kernel,
            out_shape=jax.ShapeDtypeStruct((2, out_rows * COLS, CH), BF16),
            in_specs=[pl.BlockSpec(memory_space=pltpu.SMEM)] + [vmem] * (len(operands) - 1),
            out_specs=vmem,
            scratch_shapes=[pltpu.VMEM((2 * tall * COLS, 3 * CH), BF16)],
            compiler_params=pltpu.CompilerParams(vmem_limit_bytes=VMEM_LIMIT),
        )(*operands)

    return call


def phase_kernel(phase, decoder, doubled=False, mated=False, shared=False):
    kinds = 3 if decoder else 2

    def kernel(*refs):
        refs = list(refs)
        info = refs.pop(0)
        xs = [refs.pop(0) for _ in range(6 if doubled else 3)]
        if mated:
            straight, mate, far = xs
            if shared:
                mate = mate.at[2 * BLOCK : 3 * BLOCK]
            own_rows = straight.at[2 * BLOCK : 3 * BLOCK] if shared else straight
        if decoder:
            if shared:
                skip_narrow = straight.at[0 : 2 * BLOCK]
            else:
                skips = [refs.pop(0) for _ in range(3)]
                skip_narrow = skips[1].at[0 : 2 * BLOCK]
                skip_wide = [skips[0], skips[1].at[2 * BLOCK : 3 * BLOCK], skips[2]]
        bias = refs.pop(0)
        weights = [refs.pop(0) for _ in range(6 if doubled else 2 * kinds)]
        prev0 = refs.pop(0)
        out0 = refs.pop(0)
        out1 = refs.pop(0)
        work = refs.pop(0)
        if decoder:
            skip_work = refs.pop(0)

        active = (info[0] == phase).astype(jnp.int32)
        top = info[1]

        @pl.when(active == 0)
        def _():
            out0[...] = prev0[...]
            out1[...] = prev0[2 * BLOCK : 3 * BLOCK]

        def compute(weights):
            def piece(index):
                if mated:
                    if index == 1:
                        return own_rows[...].astype(F32)
                    sides = (far, mate) if index == 0 else (mate, far)
                    return jnp.where(
                        info[3] == 0, sides[0][...].astype(F32), sides[1][...].astype(F32)
                    )
                value = xs[index][...].astype(F32)
                if doubled:
                    value = jnp.where(info[2] == 0, value, xs[index + 3][...].astype(F32))
                return value

            for index in range(3):
                value = piece(index)
                spread(work, index * BLOCK, value, ROWS)
                if shared:
                    spread(skip_work, index * BLOCK, value, ROWS)
            if decoder and not shared:
                for index, ref in enumerate(skip_wide):
                    spread(skip_work, index * BLOCK, ref[...].astype(F32), ROWS)
            for section in range(2):
                base = section * kinds
                rows = 10 - 4 * section
                start = 2 * section - 3
                total = conv(work, weights[base], rows)
                if decoder:
                    total = total + conv(skip_work, weights[base + 2], rows)
                value = finish(total, bias[2 * section : 2 * section + 1, :], rows, top + start)
                spread(work, 0, value, rows)
                if decoder and section == 0:
                    spread(skip_work, 0, skip_narrow[...].astype(F32), 2 * ROWS)
                value = finish(
                    conv(work, weights[base + 1], rows - 2),
                    bias[2 * section + 1 : 2 * section + 2, :],
                    rows - 2,
                    top + start + 1,
                )
                if section == 0:
                    out0[0 : 2 * BLOCK] = value.astype(BF16)
                    spread(work, 0, value, rows - 2)
                else:
                    out0[2 * BLOCK : 3 * BLOCK] = value.astype(BF16)
                    out1[...] = value.astype(BF16)

        if doubled:
            mine, taken, passed = weights[0:2], weights[2:4], weights[4:6]
            for parity in range(2):
                for core in range(2):
                    remote = (
                        [taken[0], passed[1]] if core == 0 else [passed[0], taken[1]]
                    )

                    @pl.when((active != 0) & (info[5] == parity) & (info[3] == core))
                    def _():
                        compute(mine + remote if parity == 0 else remote + mine)
        else:

            @pl.when(active != 0)
            def _():
                compute(weights)

    def call(info, xs, skips, bias, weights, prev0):
        operands = [info, *xs, *skips, bias, *weights, prev0]
        vmem = pl.BlockSpec(memory_space=pltpu.VMEM)
        specs = [pl.BlockSpec(memory_space=pltpu.SMEM)] + [vmem] * (len(operands) - 1)
        scratch = [pltpu.VMEM((3 * BLOCK, 3 * CH), BF16)]
        if decoder:
            scratch.append(pltpu.VMEM((3 * BLOCK, 3 * CH), BF16))
        return pl.pallas_call(
            kernel,
            out_shape=(
                jax.ShapeDtypeStruct((3 * BLOCK, CH), BF16),
                jax.ShapeDtypeStruct((BLOCK, CH), BF16),
            ),
            in_specs=specs,
            out_specs=(vmem, vmem),
            scratch_shapes=scratch,
            compiler_params=pltpu.CompilerParams(vmem_limit_bytes=VMEM_LIMIT),
            name="decode" if decoder else "encode",
        )(*operands)

    return call


def body(images, conv_first, conv_skip, conv_second, bias_first, bias_second):
    section = lax.axis_index("section")
    strip = lax.axis_index("strip")
    core = strip % 2
    parity = section % 2
    group = section // 2
    micro = jnp.where(group % 2 == 0, parity, 1 - parity)
    info = jnp.stack([group, strip * ROWS, micro, core, section, parity]).astype(jnp.int32)
    images, info, core_zero, even, group_zero, micro_zero = lax.optimization_barrier(
        (images, info, core == 0, parity == 0, group == 0, micro == 0)
    )
    own = [w.reshape(TAPS, CH) for w in (conv_first[0], conv_second[0], conv_skip[0])]
    decoders = range(SECTIONS // 2, SECTIONS)
    pairs_from = range(2, SECTIONS)
    cores = [(i, i ^ 1) for i in range(STRIPS)]

    def shift_in_section(block, which, shift):
        return lax.ppermute(
            block,
            JOINT,
            [
                (which * STRIPS + p, which * STRIPS + p + shift)
                for p in range(STRIPS)
                if 0 <= p + shift < STRIPS
            ],
        )

    def partner(block, sections=range(SECTIONS)):
        return lax.ppermute(block, "section", [(i, i ^ 1) for i in sections])

    both = jnp.concatenate([bias_first, bias_second], axis=0)
    image = images.reshape(2, BLOCK, CH)
    below = shift_in_section(image, 0, -1)
    above = shift_in_section(image, 0, 1)
    taken = [
        lax.ppermute(
            own[c],
            JOINT,
            [
                (i * STRIPS + p, (i ^ 1) * STRIPS + p)
                for i in pairs_from
                for p in range(c, STRIPS, 2)
            ],
        )
        for c in range(2)
    ]

    wide = single_kernel(0, 4)(info, (above, image, below), both, own[0], own[1])
    handed = lax.ppermute(wide, JOINT, [(p, STRIPS + p) for p in range(STRIPS)])
    close = single_kernel(1, 2)(info, (handed,), both, own[0], own[1])
    xs = [None] * 6
    for shift in (1, -1, 0):
        for to in range(2):
            xs[3 * to + 1 - shift] = lax.ppermute(
                close[to],
                JOINT,
                [
                    (STRIPS + p, place(1, to) * STRIPS + p + shift)
                    for p in range(STRIPS)
                    if 0 <= p + shift < STRIPS
                ],
            )
    other = partner(both)
    skip_weight = partner(own[2], decoders)
    give = jnp.where(even, wide[1], jnp.concatenate([close[0], close[0]], axis=0))
    got = partner(give, range(2))
    level = jnp.where(
        even,
        jnp.concatenate([wide[0], got[:BLOCK]], axis=0),
        jnp.concatenate([got, close[1]], axis=0),
    )

    passed = [
        lax.ppermute(
            taken[c],
            JOINT,
            [
                (i * STRIPS + p, i * STRIPS + (p ^ 1))
                for i in pairs_from
                for p in range(c, STRIPS, 2)
            ],
        )
        for c in range(2)
    ]
    bias = jnp.where(
        even,
        jnp.concatenate([both, other], axis=0),
        jnp.concatenate([other, both], axis=0),
    )

    def in_order(mine, remote):
        return jnp.where(even, mine, remote), jnp.where(even, remote, mine)

    def by_core(at_zero, at_one):
        return jnp.where(core_zero, at_zero, at_one)

    by_kind = [
        in_order(own[0], by_core(taken[0], passed[0])),
        in_order(own[1], by_core(passed[1], taken[1])),
        in_order(own[2], skip_weight),
    ]
    all_weights = [pair[0] for pair in by_kind] + [pair[1] for pair in by_kind]
    encode_weights = all_weights[0:2] + all_weights[3:5]

    kept = jnp.zeros((3 * BLOCK, CH), BF16)
    middle = GROUPS // 2

    def onward(last, phase, centre=None):
        following = phase + 1
        if phase % 2:
            straight = send(last if centre is None else centre, [(phase, following, 0)])
            far = lax.ppermute(
                last,
                JOINT,
                [
                    (
                        place(phase, m) * STRIPS + p + (1 if p % 2 else -1),
                        place(following, m) * STRIPS + p,
                    )
                    for m in range(2)
                    for p in range(1, STRIPS - 1)
                ],
            )
        else:
            down = send(last, [(phase, following, 1)])
            up = send(last, [(phase, following, -1)])
            return (down, send(last, [(phase, following, 0)]), up)
        mate = lax.ppermute(
            straight,
            JOINT,
            [
                (place(g, m) * STRIPS + a, place(g, m) * STRIPS + b)
                for g in range(2, GROUPS, 2)
                for m in range(2)
                for a, b in cores
            ],
        )
        return (straight, mate, far)

    for phase in range(1, middle):
        encode = phase_kernel(phase, False, doubled=phase == 1, mated=phase % 2 == 0)
        kept, last = encode(
            info,
            xs,
            (),
            bias,
            [*own[:2], *taken, *passed] if phase == 1 else encode_weights,
            kept,
        )
        xs = onward(last, phase, kept if phase + 1 == middle else None)
        if phase == middle - 2:
            mirror = [(g, GROUPS - 1 - g) for g in range(middle - 1)]
            kept = jnp.where(group_zero, level, kept)
            last = jnp.where(group_zero, level[2 * BLOCK :], last)
            late = tuple(
                send(kept if shift == 0 else last, [(a, b, shift) for a, b in mirror])
                for shift in (1, 0, -1)
            )
    for phase in range(middle, GROUPS):
        shared = phase == middle
        decode = phase_kernel(phase, True, mated=phase % 2 == 0, shared=shared)
        kept, last = decode(
            info, xs, () if shared else late, bias, all_weights, kept
        )
        if phase + 1 < GROUPS:
            xs = onward(last, phase)

    inner = kept[BLOCK // 2 : BLOCK // 2 + BLOCK]
    mine = jnp.where(even, inner, last)
    theirs = partner(jnp.where(even, last, inner))
    result = jnp.where(
        micro_zero, jnp.stack([mine, theirs]), jnp.stack([theirs, mine])
    )
    return result.reshape(1, 2, ROWS, COLS, CH)


def solution(mesh):
    placed = (
        P(None, "strip", None, None),
        P("section", None, None, None),
        P("section", None, None, None),
        P("section", None, None, None),
        P("section", None),
        P("section", None),
    )

    return jax.shard_map(
        body,
        mesh=mesh,
        in_specs=placed,
        out_specs=P("section", None, "strip", None, None),
        check_vma=False,
    )
```

```python
import jax
import jax.numpy as jnp
from jax import lax
from jax.experimental import pallas as pl
from jax.experimental.pallas import tpu as pltpu
from jax.sharding import PartitionSpec as P


BF16 = jnp.bfloat16
F32 = jnp.float32
ROWS = 4
COLS = 32
CH = 256
BLOCK = ROWS * COLS
TAPS = 9 * CH
SECTIONS = 16
STRIPS = 32
HEIGHT = ROWS * STRIPS
GROUPS = SECTIONS // 2
JOINT = ("section", "strip")
VMEM_LIMIT = 16 * 1024 * 1024


def place(group, micro):
    first = 4 * (group // 2)
    return first + (micro if group % 2 == 0 else 3 - micro)


def route(moves):
    pairs = []
    for source, target, shift in moves:
        for micro in range(2):
            for strip in range(STRIPS):
                if 0 <= strip + shift < STRIPS:
                    pairs.append(
                        (
                            place(source, micro) * STRIPS + strip,
                            place(target, micro) * STRIPS + strip + shift,
                        )
                    )
    return pairs


def send(block, moves):
    return lax.ppermute(block, JOINT, route(moves))


def spread(dest, at, value, rows):
    size = rows * COLS
    column = lax.broadcasted_iota(jnp.int32, (size, CH), 0) & (COLS - 1)
    left = jnp.where(column == 0, 0.0, pltpu.roll(value, 1, 0))
    right = jnp.where(column == COLS - 1, 0.0, pltpu.roll(value, size - 1, 0))
    dest[at : at + size, 0:CH] = left.astype(BF16)
    dest[at : at + size, CH : 2 * CH] = value.astype(BF16)
    dest[at : at + size, 2 * CH : 3 * CH] = right.astype(BF16)


def conv(source, weight, rows):
    size = rows * COLS
    total = None
    for tap in range(3):
        part = jnp.dot(
            source[tap * COLS : tap * COLS + size, :],
            weight[tap * 3 * CH : (tap + 1) * 3 * CH, :],
            preferred_element_type=F32,
        )
        total = part if total is None else total + part
    return total


def finish(total, bias, rows, first, period=None):
    size = rows * COLS
    value = jnp.maximum(total + bias, 0.0)
    row = lax.broadcasted_iota(jnp.int32, (size, CH), 0) >> 5
    if period is not None:
        row = jnp.where(row < period, row, row - period)
    row = row + first
    value = jnp.where((row >= 0) & (row < HEIGHT), value, 0.0)
    return value.astype(BF16).astype(F32)


def single_kernel(which, halo):
    tall = ROWS + 2 * halo
    out_rows = tall - 4

    def kernel(info, *refs):
        blocks = refs[:-5]
        bias, first, second, out, work = refs[-5:]

        @pl.when(info[4] != which)
        def _():
            out[...] = jnp.zeros(out.shape, BF16)

        @pl.when(info[4] == which)
        def _():
            for micro in range(2):
                at = micro * tall * COLS
                for ref in blocks:
                    rows = ref.shape[1] // COLS
                    spread(work, at, ref[micro].astype(F32), rows)
                    at += rows * COLS
            top = info[1] - halo + 1
            value = finish(conv(work, first, 2 * tall - 2), bias[0:1, :], 2 * tall - 2, top, tall)
            spread(work, 0, value, 2 * tall - 2)
            value = finish(conv(work, second, 2 * tall - 4), bias[1:2, :], 2 * tall - 4, top + 1, tall)
            value = value.astype(BF16)
            for micro in range(2):
                at = micro * tall * COLS
                out[micro] = value[at : at + out_rows * COLS]

    def call(info, blocks, bias, first, second):
        vmem = pl.BlockSpec(memory_space=pltpu.VMEM)
        operands = [info, *blocks, bias, first, second]
        return pl.pallas_call(
            kernel,
            out_shape=jax.ShapeDtypeStruct((2, out_rows * COLS, CH), BF16),
            in_specs=[pl.BlockSpec(memory_space=pltpu.SMEM)] + [vmem] * (len(operands) - 1),
            out_specs=vmem,
            scratch_shapes=[pltpu.VMEM((2 * tall * COLS, 3 * CH), BF16)],
            compiler_params=pltpu.CompilerParams(vmem_limit_bytes=VMEM_LIMIT),
        )(*operands)

    return call


def phase_kernel(phase, decoder, doubled=False, mated=False, shared=False):
    kinds = 3 if decoder else 2

    def kernel(*refs):
        refs = list(refs)
        info = refs.pop(0)
        xs = [refs.pop(0) for _ in range(6 if doubled else 3)]
        if mated:
            straight, mate, far = xs
            if shared:
                mate = mate.at[2 * BLOCK : 3 * BLOCK]
            own_rows = straight.at[2 * BLOCK : 3 * BLOCK] if shared else straight
        if decoder:
            if shared:
                skip_narrow = straight.at[0 : 2 * BLOCK]
            else:
                skips = [refs.pop(0) for _ in range(3)]
                skip_narrow = skips[1].at[0 : 2 * BLOCK]
                skip_wide = [skips[0], skips[1].at[2 * BLOCK : 3 * BLOCK], skips[2]]
        bias = refs.pop(0)
        weights = [refs.pop(0) for _ in range(6 if doubled else 2 * kinds)]
        prev0 = refs.pop(0)
        out0 = refs.pop(0)
        out1 = refs.pop(0)
        work = refs.pop(0)
        if decoder:
            skip_work = refs.pop(0)

        active = (info[0] == phase).astype(jnp.int32)
        top = info[1]

        @pl.when(active == 0)
        def _():
            out0[...] = prev0[...]
            out1[...] = prev0[2 * BLOCK : 3 * BLOCK]

        def compute(weights):
            def piece(index):
                if mated:
                    if index == 1:
                        return own_rows[...].astype(F32)
                    sides = (far, mate) if index == 0 else (mate, far)
                    return jnp.where(
                        info[3] == 0, sides[0][...].astype(F32), sides[1][...].astype(F32)
                    )
                value = xs[index][...].astype(F32)
                if doubled:
                    value = jnp.where(info[2] == 0, value, xs[index + 3][...].astype(F32))
                return value

            for index in range(3):
                value = piece(index)
                spread(work, index * BLOCK, value, ROWS)
                if shared:
                    spread(skip_work, index * BLOCK, value, ROWS)
            if decoder and not shared:
                for index, ref in enumerate(skip_wide):
                    spread(skip_work, index * BLOCK, ref[...].astype(F32), ROWS)
            for section in range(2):
                base = section * kinds
                rows = 10 - 4 * section
                start = 2 * section - 3
                total = conv(work, weights[base], rows)
                if decoder:
                    total = total + conv(skip_work, weights[base + 2], rows)
                value = finish(total, bias[2 * section : 2 * section + 1, :], rows, top + start)
                spread(work, 0, value, rows)
                if decoder and section == 0:
                    spread(skip_work, 0, skip_narrow[...].astype(F32), 2 * ROWS)
                value = finish(
                    conv(work, weights[base + 1], rows - 2),
                    bias[2 * section + 1 : 2 * section + 2, :],
                    rows - 2,
                    top + start + 1,
                )
                if section == 0:
                    out0[0 : 2 * BLOCK] = value.astype(BF16)
                    spread(work, 0, value, rows - 2)
                else:
                    out0[2 * BLOCK : 3 * BLOCK] = value.astype(BF16)
                    out1[...] = value.astype(BF16)

        if doubled:
            mine, taken, passed = weights[0:2], weights[2:4], weights[4:6]
            for parity in range(2):
                for core in range(2):
                    remote = (
                        [taken[0], passed[1]] if core == 0 else [passed[0], taken[1]]
                    )

                    @pl.when((active != 0) & (info[5] == parity) & (info[3] == core))
                    def _():
                        compute(mine + remote if parity == 0 else remote + mine)
        else:

            @pl.when(active != 0)
            def _():
                compute(weights)

    def call(info, xs, skips, bias, weights, prev0):
        operands = [info, *xs, *skips, bias, *weights, prev0]
        vmem = pl.BlockSpec(memory_space=pltpu.VMEM)
        specs = [pl.BlockSpec(memory_space=pltpu.SMEM)] + [vmem] * (len(operands) - 1)
        scratch = [pltpu.VMEM((3 * BLOCK, 3 * CH), BF16)]
        if decoder:
            scratch.append(pltpu.VMEM((3 * BLOCK, 3 * CH), BF16))
        return pl.pallas_call(
            kernel,
            out_shape=(
                jax.ShapeDtypeStruct((3 * BLOCK, CH), BF16),
                jax.ShapeDtypeStruct((BLOCK, CH), BF16),
            ),
            in_specs=specs,
            out_specs=(vmem, vmem),
            scratch_shapes=scratch,
            compiler_params=pltpu.CompilerParams(vmem_limit_bytes=VMEM_LIMIT),
            name="decode" if decoder else "encode",
        )(*operands)

    return call


def body(images, conv_first, conv_skip, conv_second, bias_first, bias_second):
    section = lax.axis_index("section")
    strip = lax.axis_index("strip")
    core = strip % 2
    parity = section % 2
    group = section // 2
    micro = jnp.where(group % 2 == 0, parity, 1 - parity)
    info = jnp.stack([group, strip * ROWS, micro, core, section, parity]).astype(jnp.int32)
    images, info, core_zero, even, group_zero, micro_zero = lax.optimization_barrier(
        (images, info, core == 0, parity == 0, group == 0, micro == 0)
    )
    own = [w.reshape(TAPS, CH) for w in (conv_first[0], conv_second[0], conv_skip[0])]
    decoders = range(SECTIONS // 2, SECTIONS)
    pairs_from = range(2, SECTIONS)
    cores = [(i, i ^ 1) for i in range(STRIPS)]

    def shift_in_section(block, which, shift):
        return lax.ppermute(
            block,
            JOINT,
            [
                (which * STRIPS + p, which * STRIPS + p + shift)
                for p in range(STRIPS)
                if 0 <= p + shift < STRIPS
            ],
        )

    def partner(block, sections=range(SECTIONS)):
        return lax.ppermute(block, "section", [(i, i ^ 1) for i in sections])

    both = jnp.concatenate([bias_first, bias_second], axis=0)
    image = images.reshape(2, BLOCK, CH)
    below = shift_in_section(image, 0, -1)
    above = shift_in_section(image, 0, 1)
    taken = [
        lax.ppermute(
            own[c],
            JOINT,
            [
                (i * STRIPS + p, (i ^ 1) * STRIPS + p)
                for i in pairs_from
                for p in range(c, STRIPS, 2)
            ],
        )
        for c in range(2)
    ]

    wide = single_kernel(0, 4)(info, (above, image, below), both, own[0], own[1])
    handed = lax.ppermute(wide, JOINT, [(p, STRIPS + p) for p in range(STRIPS)])
    close = single_kernel(1, 2)(info, (handed,), both, own[0], own[1])
    xs = [None] * 6
    for shift in (1, -1, 0):
        for to in range(2):
            xs[3 * to + 1 - shift] = lax.ppermute(
                close[to],
                JOINT,
                [
                    (STRIPS + p, place(1, to) * STRIPS + p + shift)
                    for p in range(STRIPS)
                    if 0 <= p + shift < STRIPS
                ],
            )
    other = partner(both)
    skip_weight = partner(own[2], decoders)
    give = jnp.where(even, wide[1], jnp.concatenate([close[0], close[0]], axis=0))
    got = partner(give, range(2))
    level = jnp.where(
        even,
        jnp.concatenate([wide[0], got[:BLOCK]], axis=0),
        jnp.concatenate([got, close[1]], axis=0),
    )

    passed = [
        lax.ppermute(
            taken[c],
            JOINT,
            [
                (i * STRIPS + p, i * STRIPS + (p ^ 1))
                for i in pairs_from
                for p in range(c, STRIPS, 2)
            ],
        )
        for c in range(2)
    ]
    bias = jnp.where(
        even,
        jnp.concatenate([both, other], axis=0),
        jnp.concatenate([other, both], axis=0),
    )

    def in_order(mine, remote):
        return jnp.where(even, mine, remote), jnp.where(even, remote, mine)

    def by_core(at_zero, at_one):
        return jnp.where(core_zero, at_zero, at_one)

    by_kind = [
        in_order(own[0], by_core(taken[0], passed[0])),
        in_order(own[1], by_core(passed[1], taken[1])),
        in_order(own[2], skip_weight),
    ]
    all_weights = [pair[0] for pair in by_kind] + [pair[1] for pair in by_kind]
    encode_weights = all_weights[0:2] + all_weights[3:5]

    kept = jnp.zeros((3 * BLOCK, CH), BF16)
    middle = GROUPS // 2

    def onward(last, phase, centre=None):
        following = phase + 1
        straight = send(last if centre is None else centre, [(phase, following, 0)])
        far = lax.ppermute(
            last,
            JOINT,
            [
                (
                    place(phase, m) * STRIPS + p + (1 if p % 2 else -1),
                    place(following, m) * STRIPS + p,
                )
                for m in range(2)
                for p in range(1, STRIPS - 1)
            ],
        )
        mate = lax.ppermute(
            straight,
            JOINT,
            [
                (place(g, m) * STRIPS + a, place(g, m) * STRIPS + b)
                for g in range(2 + following % 2, GROUPS, 2)
                for m in range(2)
                for a, b in cores
            ],
        )
        return (straight, mate, far)

    for phase in range(1, middle):
        encode = phase_kernel(phase, False, doubled=phase == 1, mated=phase > 1)
        kept, last = encode(
            info,
            xs,
            (),
            bias,
            [*own[:2], *taken, *passed] if phase == 1 else encode_weights,
            kept,
        )
        xs = onward(last, phase, kept if phase + 1 == middle else None)
        if phase == middle - 2:
            mirror = [(g, GROUPS - 1 - g) for g in range(middle - 1)]
            kept = jnp.where(group_zero, level, kept)
            last = jnp.where(group_zero, level[2 * BLOCK :], last)
            late = tuple(
                send(kept if shift == 0 else last, [(a, b, shift) for a, b in mirror])
                for shift in (1, 0, -1)
            )
    for phase in range(middle, GROUPS):
        shared = phase == middle
        decode = phase_kernel(phase, True, mated=phase > 1, shared=shared)
        kept, last = decode(
            info, xs, () if shared else late, bias, all_weights, kept
        )
        if phase + 1 < GROUPS:
            xs = onward(last, phase)

    inner = kept[BLOCK // 2 : BLOCK // 2 + BLOCK]
    mine = jnp.where(even, inner, last)
    theirs = partner(jnp.where(even, last, inner))
    result = jnp.where(
        micro_zero, jnp.stack([mine, theirs]), jnp.stack([theirs, mine])
    )
    return result.reshape(1, 2, ROWS, COLS, CH)


def solution(mesh):
    placed = (
        P(None, "strip", None, None),
        P("section", None, None, None),
        P("section", None, None, None),
        P("section", None, None, None),
        P("section", None),
        P("section", None),
    )

    return jax.shard_map(
        body,
        mesh=mesh,
        in_specs=placed,
        out_specs=P("section", None, "strip", None, None),
        check_vma=False,
    )
```

```python
import jax
import jax.numpy as jnp
from jax import lax
from jax.experimental import pallas as pl
from jax.experimental.pallas import tpu as pltpu
from jax.sharding import PartitionSpec as P


BF16 = jnp.bfloat16
F32 = jnp.float32
ROWS = 4
COLS = 32
CH = 256
BLOCK = ROWS * COLS
TAPS = 9 * CH
SECTIONS = 16
STRIPS = 32
HEIGHT = ROWS * STRIPS
GROUPS = SECTIONS // 2
JOINT = ("section", "strip")
VMEM_LIMIT = 16 * 1024 * 1024


def place(group, micro):
    first = 4 * (group // 2)
    return first + (micro if group % 2 == 0 else 3 - micro)


def route(moves):
    pairs = []
    for source, target, shift in moves:
        for micro in range(2):
            for strip in range(STRIPS):
                if 0 <= strip + shift < STRIPS:
                    pairs.append(
                        (
                            place(source, micro) * STRIPS + strip,
                            place(target, micro) * STRIPS + strip + shift,
                        )
                    )
    return pairs


def send(block, moves):
    return lax.ppermute(block, JOINT, route(moves))


def spread(dest, at, value, rows):
    size = rows * COLS
    column = lax.broadcasted_iota(jnp.int32, (size, CH), 0) & (COLS - 1)
    left = jnp.where(column == 0, 0.0, pltpu.roll(value, 1, 0))
    right = jnp.where(column == COLS - 1, 0.0, pltpu.roll(value, size - 1, 0))
    dest[at : at + size, 0:CH] = left.astype(BF16)
    dest[at : at + size, CH : 2 * CH] = value.astype(BF16)
    dest[at : at + size, 2 * CH : 3 * CH] = right.astype(BF16)


def conv(source, weight, rows):
    size = rows * COLS
    total = None
    for tap in range(3):
        part = jnp.dot(
            source[tap * COLS : tap * COLS + size, :],
            weight[tap * 3 * CH : (tap + 1) * 3 * CH, :],
            preferred_element_type=F32,
        )
        total = part if total is None else total + part
    return total


def finish(total, bias, rows, first, period=None):
    size = rows * COLS
    value = jnp.maximum(total + bias, 0.0)
    row = lax.broadcasted_iota(jnp.int32, (size, CH), 0) >> 5
    if period is not None:
        row = jnp.where(row < period, row, row - period)
    row = row + first
    value = jnp.where((row >= 0) & (row < HEIGHT), value, 0.0)
    return value.astype(BF16).astype(F32)


def single_kernel(which, halo):
    tall = ROWS + 2 * halo
    out_rows = tall - 4

    def kernel(info, *refs):
        blocks = refs[:-5]
        bias, first, second, out, work = refs[-5:]

        @pl.when(info[4] != which)
        def _():
            out[...] = jnp.zeros(out.shape, BF16)

        @pl.when(info[4] == which)
        def _():
            for micro in range(2):
                at = micro * tall * COLS
                for ref in blocks:
                    rows = ref.shape[1] // COLS
                    spread(work, at, ref[micro].astype(F32), rows)
                    at += rows * COLS
            top = info[1] - halo + 1
            value = finish(conv(work, first, 2 * tall - 2), bias[0:1, :], 2 * tall - 2, top, tall)
            spread(work, 0, value, 2 * tall - 2)
            value = finish(conv(work, second, 2 * tall - 4), bias[1:2, :], 2 * tall - 4, top + 1, tall)
            value = value.astype(BF16)
            for micro in range(2):
                at = micro * tall * COLS
                out[micro] = value[at : at + out_rows * COLS]

    def call(info, blocks, bias, first, second):
        vmem = pl.BlockSpec(memory_space=pltpu.VMEM)
        operands = [info, *blocks, bias, first, second]
        return pl.pallas_call(
            kernel,
            out_shape=jax.ShapeDtypeStruct((2, out_rows * COLS, CH), BF16),
            in_specs=[pl.BlockSpec(memory_space=pltpu.SMEM)] + [vmem] * (len(operands) - 1),
            out_specs=vmem,
            scratch_shapes=[pltpu.VMEM((2 * tall * COLS, 3 * CH), BF16)],
            compiler_params=pltpu.CompilerParams(vmem_limit_bytes=VMEM_LIMIT),
        )(*operands)

    return call


def phase_kernel(phase, decoder, doubled=False, mated=False, shared=False):
    kinds = 3 if decoder else 2

    def kernel(*refs):
        refs = list(refs)
        info = refs.pop(0)
        xs = [refs.pop(0) for _ in range(6 if doubled else 4 if shared else 3)]
        if mated:
            own_rows, mate, far = xs[:3]
        if decoder:
            if shared:
                skip_narrow = xs[3]
            else:
                skips = [refs.pop(0) for _ in range(3)]
                skip_narrow = skips[1].at[0 : 2 * BLOCK]
                skip_wide = [skips[0], skips[1].at[2 * BLOCK : 3 * BLOCK], skips[2]]
        bias = refs.pop(0)
        weights = [refs.pop(0) for _ in range(6 if doubled else 2 * kinds)]
        prev0 = refs.pop(0)
        out0 = refs.pop(0)
        out1 = refs.pop(0)
        work = refs.pop(0)
        if decoder:
            skip_work = refs.pop(0)

        active = (info[0] == phase).astype(jnp.int32)
        top = info[1]

        @pl.when(active == 0)
        def _():
            out0[...] = prev0[...]
            out1[...] = prev0[2 * BLOCK : 3 * BLOCK]

        def compute(weights):
            def piece(index):
                if mated:
                    if index == 1:
                        return own_rows[...].astype(F32)
                    sides = (far, mate) if index == 0 else (mate, far)
                    return jnp.where(
                        info[3] == 0, sides[0][...].astype(F32), sides[1][...].astype(F32)
                    )
                value = xs[index][...].astype(F32)
                if doubled:
                    value = jnp.where(info[2] == 0, value, xs[index + 3][...].astype(F32))
                return value

            for index in range(3):
                value = piece(index)
                spread(work, index * BLOCK, value, ROWS)
                if shared:
                    spread(skip_work, index * BLOCK, value, ROWS)
            if decoder and not shared:
                for index, ref in enumerate(skip_wide):
                    spread(skip_work, index * BLOCK, ref[...].astype(F32), ROWS)
            for section in range(2):
                base = section * kinds
                rows = 10 - 4 * section
                start = 2 * section - 3
                total = conv(work, weights[base], rows)
                if decoder:
                    total = total + conv(skip_work, weights[base + 2], rows)
                value = finish(total, bias[2 * section : 2 * section + 1, :], rows, top + start)
                spread(work, 0, value, rows)
                if decoder and section == 0:
                    spread(skip_work, 0, skip_narrow[...].astype(F32), 2 * ROWS)
                value = finish(
                    conv(work, weights[base + 1], rows - 2),
                    bias[2 * section + 1 : 2 * section + 2, :],
                    rows - 2,
                    top + start + 1,
                )
                if section == 0:
                    out0[0 : 2 * BLOCK] = value.astype(BF16)
                    spread(work, 0, value, rows - 2)
                else:
                    out0[2 * BLOCK : 3 * BLOCK] = value.astype(BF16)
                    out1[...] = value.astype(BF16)

        if doubled:
            mine, taken, passed = weights[0:2], weights[2:4], weights[4:6]
            for parity in range(2):
                for core in range(2):
                    remote = (
                        [taken[0], passed[1]] if core == 0 else [passed[0], taken[1]]
                    )

                    @pl.when((active != 0) & (info[5] == parity) & (info[3] == core))
                    def _():
                        compute(mine + remote if parity == 0 else remote + mine)
        else:

            @pl.when(active != 0)
            def _():
                compute(weights)

    def call(info, xs, skips, bias, weights, prev0):
        operands = [info, *xs, *skips, bias, *weights, prev0]
        vmem = pl.BlockSpec(memory_space=pltpu.VMEM)
        specs = [pl.BlockSpec(memory_space=pltpu.SMEM)] + [vmem] * (len(operands) - 1)
        scratch = [pltpu.VMEM((3 * BLOCK, 3 * CH), BF16)]
        if decoder:
            scratch.append(pltpu.VMEM((3 * BLOCK, 3 * CH), BF16))
        return pl.pallas_call(
            kernel,
            out_shape=(
                jax.ShapeDtypeStruct((3 * BLOCK, CH), BF16),
                jax.ShapeDtypeStruct((BLOCK, CH), BF16),
            ),
            in_specs=specs,
            out_specs=(vmem, vmem),
            scratch_shapes=scratch,
            compiler_params=pltpu.CompilerParams(vmem_limit_bytes=VMEM_LIMIT),
            name="decode" if decoder else "encode",
        )(*operands)

    return call


def body(images, conv_first, conv_skip, conv_second, bias_first, bias_second):
    section = lax.axis_index("section")
    strip = lax.axis_index("strip")
    core = strip % 2
    parity = section % 2
    group = section // 2
    micro = jnp.where(group % 2 == 0, parity, 1 - parity)
    info = jnp.stack([group, strip * ROWS, micro, core, section, parity]).astype(jnp.int32)
    images, info, core_zero, even, group_zero, micro_zero = lax.optimization_barrier(
        (images, info, core == 0, parity == 0, group == 0, micro == 0)
    )
    own = [w.reshape(TAPS, CH) for w in (conv_first[0], conv_second[0], conv_skip[0])]
    decoders = range(SECTIONS // 2, SECTIONS)
    pairs_from = range(2, SECTIONS)
    cores = [(i, i ^ 1) for i in range(STRIPS)]

    def shift_in_section(block, which, shift):
        return lax.ppermute(
            block,
            JOINT,
            [
                (which * STRIPS + p, which * STRIPS + p + shift)
                for p in range(STRIPS)
                if 0 <= p + shift < STRIPS
            ],
        )

    def partner(block, sections=range(SECTIONS)):
        return lax.ppermute(block, "section", [(i, i ^ 1) for i in sections])

    both = jnp.concatenate([bias_first, bias_second], axis=0)
    image = images.reshape(2, BLOCK, CH)
    below = shift_in_section(image, 0, -1)
    above = shift_in_section(image, 0, 1)
    taken = [
        lax.ppermute(
            own[c],
            JOINT,
            [
                (i * STRIPS + p, (i ^ 1) * STRIPS + p)
                for i in pairs_from
                for p in range(c, STRIPS, 2)
            ],
        )
        for c in range(2)
    ]

    wide = single_kernel(0, 4)(info, (above, image, below), both, own[0], own[1])
    handed = lax.ppermute(wide, JOINT, [(p, STRIPS + p) for p in range(STRIPS)])
    close = single_kernel(1, 2)(info, (handed,), both, own[0], own[1])
    xs = [None] * 6
    for shift in (1, -1, 0):
        for to in range(2):
            xs[3 * to + 1 - shift] = lax.ppermute(
                close[to],
                JOINT,
                [
                    (STRIPS + p, place(1, to) * STRIPS + p + shift)
                    for p in range(STRIPS)
                    if 0 <= p + shift < STRIPS
                ],
            )
    other = partner(both)
    skip_weight = partner(own[2], decoders)
    give = jnp.where(even, wide[1], jnp.concatenate([close[0], close[0]], axis=0))
    got = partner(give, range(2))
    level = jnp.where(
        even,
        jnp.concatenate([wide[0], got[:BLOCK]], axis=0),
        jnp.concatenate([got, close[1]], axis=0),
    )

    passed = [
        lax.ppermute(
            taken[c],
            JOINT,
            [
                (i * STRIPS + p, i * STRIPS + (p ^ 1))
                for i in pairs_from
                for p in range(c, STRIPS, 2)
            ],
        )
        for c in range(2)
    ]
    bias = jnp.where(
        even,
        jnp.concatenate([both, other], axis=0),
        jnp.concatenate([other, both], axis=0),
    )

    def in_order(mine, remote):
        return jnp.where(even, mine, remote), jnp.where(even, remote, mine)

    def by_core(at_zero, at_one):
        return jnp.where(core_zero, at_zero, at_one)

    by_kind = [
        in_order(own[0], by_core(taken[0], passed[0])),
        in_order(own[1], by_core(passed[1], taken[1])),
        in_order(own[2], skip_weight),
    ]
    all_weights = [pair[0] for pair in by_kind] + [pair[1] for pair in by_kind]
    encode_weights = all_weights[0:2] + all_weights[3:5]

    kept = jnp.zeros((3 * BLOCK, CH), BF16)
    middle = GROUPS // 2

    def onward(last, phase, centre=None):
        following = phase + 1
        if phase % 2:
            straight = send(last if centre is None else centre, [(phase, following, 0)])
            far = lax.ppermute(
                last,
                JOINT,
                [
                    (
                        place(phase, m) * STRIPS + p + (1 if p % 2 else -1),
                        place(following, m) * STRIPS + p,
                    )
                    for m in range(2)
                    for p in range(1, STRIPS - 1)
                ],
            )
        else:
            down = send(last, [(phase, following, 1)])
            up = send(last, [(phase, following, -1)])
            return (down, send(last, [(phase, following, 0)]), up)
        mate = lax.ppermute(
            straight,
            JOINT,
            [
                (place(g, m) * STRIPS + a, place(g, m) * STRIPS + b)
                for g in range(2, GROUPS, 2)
                for m in range(2)
                for a, b in cores
            ],
        )
        return (straight, mate, far)

    for phase in range(1, middle):
        encode = phase_kernel(phase, False, doubled=phase == 1, mated=phase % 2 == 0)
        kept, last = encode(
            info,
            xs,
            (),
            bias,
            [*own[:2], *taken, *passed] if phase == 1 else encode_weights,
            kept,
        )
        xs = onward(last, phase)
        if phase + 1 == middle:
            xs = (*xs, send(kept[: 2 * BLOCK], [(phase, middle, 0)]))
        if phase == middle - 2:
            mirror = [(g, GROUPS - 1 - g) for g in range(middle - 1)]
            kept = jnp.where(group_zero, level, kept)
            last = jnp.where(group_zero, level[2 * BLOCK :], last)
            late = tuple(
                send(kept if shift == 0 else last, [(a, b, shift) for a, b in mirror])
                for shift in (1, 0, -1)
            )
    for phase in range(middle, GROUPS):
        shared = phase == middle
        decode = phase_kernel(phase, True, mated=phase % 2 == 0, shared=shared)
        kept, last = decode(
            info, xs, () if shared else late, bias, all_weights, kept
        )
        if phase + 1 < GROUPS:
            xs = onward(last, phase)

    inner = kept[BLOCK // 2 : BLOCK // 2 + BLOCK]
    mine = jnp.where(even, inner, last)
    theirs = partner(jnp.where(even, last, inner))
    result = jnp.where(
        micro_zero, jnp.stack([mine, theirs]), jnp.stack([theirs, mine])
    )
    return result.reshape(1, 2, ROWS, COLS, CH)


def solution(mesh):
    placed = (
        P(None, "strip", None, None),
        P("section", None, None, None),
        P("section", None, None, None),
        P("section", None, None, None),
        P("section", None),
        P("section", None),
    )

    return jax.shard_map(
        body,
        mesh=mesh,
        in_specs=placed,
        out_specs=P("section", None, "strip", None, None),
        check_vma=False,
    )
```
